256 devices in a mesh: leaf: 64 (over z, x, core), rhs: 4 (over y).
Axes of the slice: x: 4, y: 4, z: 8, core: 2. Of those that a mesh axis runs over, the one named last changes fastest.
Arguments:
- points: bfloat16 [131072, 784], P('leaf'), may hold values from -8 to 8
- vectors: bfloat16 [131072, 128], P('leaf', 'rhs'), may hold values from -6 to 6
- bases: float32 [512, 256, 64], P('leaf'), may hold values from -0.375 to 0.375
- leaf_coupling: float32 [512, 8, 64, 64], P('leaf'), may hold values from -0.75 to 0.75
- transfer: float32 [512, 64, 64], P('leaf'), may hold values from -0.75 to 0.75
- up_coupling: float32 [256, 8, 64, 64], P('leaf'), may hold values from -0.75 to 0.75
- far_leaf: int32 [512, 8], P('leaf'), may hold values from 0 to 511, as said below
- far_up: int32 [256, 8], P('leaf'), may hold values from 0 to 255, as said below
- near_lists: int32 [512, 8], P('leaf'), may hold values from -1 to 511, as said below
Outputs:
- product: float32 [131072, 128], P('leaf', 'rhs')
The draws below stay inside these ranges and needn't reach their ends.
Inputs may be any that keep to these rules, and one draw needn't show every extreme that they name: `near_lists`: row i begins with i itself; the other entries are distinct leaves j with 0 < |i - j| <= 8, or -1 for an unused slot. `far_leaf`: each row holds 8 distinct leaves, each more than 8 away from the row's own leaf in index. `far_up`: each row holds 8 distinct parents, each at least 2 away from the row's own parent in index.
All inputs are finite; a program needn't handle non-finite values.
Results may differ from the reference program's by a relative error of at most 0.0025.
Values may be sent and summed in bfloat16 or wider, within the bound.
A program may use at most 128 MiB of HBM per device.

```python
import math
import jax
import jax.numpy as jnp
from jax import lax

D = 784
LEAF_PTS = 256
RANK = 64
NRHS = 128
NEAR = 8
FAR = 8
FAR_UP = 8
LEAF_DEV = 8
LEAVES = 512
PARENTS = 256
POINTS = 131072


def draw_points(key, part):
    latent_dims = 8
    carry_rate = 0.84
    jitter_scale = 0.5
    subkeys = jax.random.split(jax.random.fold_in(key, 53), 4)
    shocks = jax.random.normal(subkeys[0], (LEAVES, latent_dims), jnp.float32)

    def advance(current, innovation):
        stepped = carry_rate * current + math.sqrt(1.0 - carry_rate * carry_rate) * innovation
        return (stepped, stepped)
    opening = shocks[0]
    unused, following = lax.scan(advance, opening, shocks[1:])
    centres = jnp.concatenate([opening[None, :], following], axis=0)
    offsets = jax.random.normal(subkeys[1], (LEAVES, LEAF_PTS, latent_dims), jnp.float32)
    jitter = jax.random.normal(subkeys[3], (POINTS, D), jnp.float32) * jitter_scale
    embedding = jax.random.normal(subkeys[2], (latent_dims, D), jnp.float32) / math.sqrt(latent_dims)
    latent = (centres[:, None, :] + offsets).reshape(POINTS, latent_dims)
    placed = jnp.dot(latent, embedding, precision=lax.Precision.HIGHEST) + jitter
    return jnp.clip(placed, -8.0, 8.0).astype(jnp.bfloat16)


def draw_near_lists(key, part):
    offsets = jnp.concatenate([jnp.arange(LEAF_DEV, dtype=jnp.int32) - LEAF_DEV, jnp.arange(LEAF_DEV, dtype=jnp.int32) + 1])
    subkeys = jax.random.split(jax.random.fold_in(key, 11), LEAVES)

    def pick_row(subkey):
        return jax.random.permutation(subkey, offsets)
    chosen = jax.vmap(pick_row)(subkeys)
    taken_count = min(NEAR - 1, 2 * LEAF_DEV)
    leaf_ids = jnp.arange(LEAVES, dtype=jnp.int32)
    others = leaf_ids[:, None] + chosen[:, :taken_count]
    others = jnp.where((others >= 0) & (others < LEAVES), others, -1).astype(jnp.int32)
    padding = -jnp.ones((LEAVES, NEAR - 1 - taken_count), jnp.int32)
    return jnp.concatenate([leaf_ids[:, None], others, padding], axis=1)


def draw_far_leaf(key, part):
    window = LEAVES - 2 * LEAF_DEV - 1
    subkeys = jax.random.split(jax.random.fold_in(key, 23), LEAVES)

    def pick_row(subkey):
        return jax.random.permutation(subkey, window)[:FAR].astype(jnp.int32)
    chosen = jax.vmap(pick_row)(subkeys)
    leaf_ids = jnp.arange(LEAVES, dtype=jnp.int32)
    return ((leaf_ids[:, None] + LEAF_DEV + 1 + chosen) % LEAVES).astype(jnp.int32)


def draw_far_up(key, part):
    window = PARENTS - 3
    subkeys = jax.random.split(jax.random.fold_in(key, 37), PARENTS)

    def pick_row(subkey):
        return jax.random.permutation(subkey, window)[:FAR_UP].astype(jnp.int32)
    chosen = jax.vmap(pick_row)(subkeys)
    parent_ids = jnp.arange(PARENTS, dtype=jnp.int32)
    return ((parent_ids[:, None] + 2 + chosen) % PARENTS).astype(jnp.int32)


def level_of(rng, shape, cuts, smallest, high):
    level, own = 1.0, jax.random.fold_in(rng, 6)
    for dim, shards_of in cuts:
        steps = jnp.exp(jax.random.uniform(jax.random.fold_in(own, dim), (shards_of,), jnp.float32, smallest / len(cuts), high / len(cuts)))
        level = level * jnp.repeat(steps, shape[dim] // shards_of).reshape([-1 if axis == dim else 1 for axis in range(len(shape))])
    return level


def noise(own_key, shape, width, limit, cuts=(), kind=jnp.bfloat16):
    values = width * jax.random.normal(own_key, shape, jnp.float32)
    if cuts:
        values = values * level_of(own_key, shape, cuts, -0.22, 0.18)
    return jnp.clip(values, -limit, limit).astype(kind)


def setup_inputs(seed: int = 0) -> dict:
    splits = jax.random.split(jax.random.key(seed), 10)
    points = draw_points(jax.random.fold_in(splits[9], 71), 0)
    vectors = noise(splits[1], (POINTS, NRHS), 1.0, 6.0, ((0, 64), (1, 4)))
    bases = noise(splits[2], (LEAVES, LEAF_PTS, RANK), LEAF_PTS ** -0.5, 0.375, ((0, 64),), jnp.float32)
    leaf_coupling = noise(splits[3], (LEAVES, FAR, RANK, RANK), RANK ** -0.5, 0.75, ((0, 64),), jnp.float32)
    transfer = noise(splits[4], (LEAVES, RANK, RANK), RANK ** -0.5, 0.75, ((0, 64),), jnp.float32)
    up_coupling = noise(splits[5], (PARENTS, FAR_UP, RANK, RANK), RANK ** -0.5, 0.75, ((0, 64),), jnp.float32)
    far_leaf = draw_far_leaf(jax.random.fold_in(splits[9], 71), 0)
    far_up = draw_far_up(jax.random.fold_in(splits[9], 71), 0)
    near_lists = draw_near_lists(jax.random.fold_in(splits[9], 71), 0)
    return dict(points=points, vectors=vectors, bases=bases, leaf_coupling=leaf_coupling, transfer=transfer, up_coupling=up_coupling, far_leaf=far_leaf, far_up=far_up, near_lists=near_lists)


HIGHEST = lax.Precision.HIGHEST


def reference(points, vectors, bases, leaf_coupling, transfer, up_coupling, far_leaf, far_up, near_lists):
    vec_float = vectors.astype(jnp.float32).reshape(LEAVES, LEAF_PTS, NRHS)
    coeffs = jnp.einsum("lpr,lpc->lrc", bases, vec_float, precision=HIGHEST)
    lifted = jnp.einsum("lba,lbc->lac", transfer, coeffs, precision=HIGHEST)
    parents = lifted.reshape(PARENTS, 2, RANK, NRHS).sum(axis=1)
    leaf_field = jnp.einsum("lkab,lkbc->lac", leaf_coupling, jnp.take(coeffs, far_leaf, axis=0), precision=HIGHEST)
    upper_field = jnp.einsum("qkab,qkbc->qac", up_coupling, jnp.take(parents, far_up, axis=0), precision=HIGHEST)
    pushed = jnp.einsum("lab,lbc->lac", transfer, jnp.repeat(upper_field, 2, axis=0), precision=HIGHEST)
    far_part = jnp.einsum("lpr,lrc->lpc", bases, leaf_field + pushed, precision=HIGHEST)
    far_part = far_part.reshape(POINTS, NRHS)
    square_sums = jnp.sum(jnp.square(points.astype(jnp.float32)), axis=1)
    offsets = jnp.arange(LEAF_PTS, dtype=jnp.int32)

    def near_leaf(leaf_index):
        slot_ids = near_lists[leaf_index]
        usable = slot_ids >= 0
        safe_ids = jnp.where(usable, slot_ids, 0).astype(jnp.int32)
        row_ids = (safe_ids[:, None] * LEAF_PTS + offsets[None, :]).reshape(-1)
        near_points = jnp.take(points, row_ids, axis=0)
        own_points = lax.dynamic_slice_in_dim(points, leaf_index * LEAF_PTS, LEAF_PTS, 0)
        own_sums = lax.dynamic_slice_in_dim(square_sums, leaf_index * LEAF_PTS, LEAF_PTS, 0)
        cross_terms = lax.dot_general(own_points, near_points, (((1,), (1,)), ((), ())), preferred_element_type=jnp.float32)
        distance = own_sums[:, None] + jnp.take(square_sums, row_ids)[None, :] - 2.0 * cross_terms
        column_mask = jnp.repeat(usable.astype(jnp.float32), LEAF_PTS)
        kernel = (jnp.exp(-distance / D) * column_mask[None, :]).astype(jnp.bfloat16)
        near_vectors = jnp.take(vectors, row_ids, axis=0)
        return jnp.dot(kernel, near_vectors, preferred_element_type=jnp.float32)

    near_part = lax.map(near_leaf, jnp.arange(LEAVES, dtype=jnp.int32)).reshape(POINTS, NRHS)
    return near_part + far_part + 0.5 * vectors.astype(jnp.float32)
```

```python
import functools
import math

import jax
import jax.numpy as jnp
from jax import lax
from jax.experimental import pallas as pl
from jax.experimental.pallas import tpu as pltpu
from jax.sharding import PartitionSpec as P

MESH = pl.DeviceIdType.MESH
F32 = jnp.float32
BF16 = jnp.bfloat16
RIDGE = 0.5
NN = (((1,), (0,)), ((), ()))
NT = (((1,), (1,)), ((), ()))


def mm(a, b, dims=NN):
    return lax.dot_general(a, b, dims, preferred_element_type=F32)


def split(w):
    high = w.astype(BF16)
    return high, (w - high.astype(F32)).astype(BF16)


def kernel(
    dims,
    pts, vt, bases, lc, tr, uc, fl, fu, nl,
    out,
    pv, hp, vall, hv, nlr, masks, bv, lv, tv, uv, gat, wl, wu, halves,
    ncol, nrow, acc, hacc, hsend, hres, asend, arecv,
    lsem, hp_s, hp_r, v_s, v_r, nl_s, nl_r, hv_s, hv_r, z_s, z_r, x_s, x_r, c_s, c_r, hs_s, hs_r, a_s, a_r,
):
    zdim, xdim, ydim = dims
    n = zdim * xdim * 2
    d = lax.axis_index("leaf")
    r = lax.axis_index("rhs")
    core = lax.rem(d, 2)
    x = lax.rem(lax.div(d, 2), xdim)
    z = lax.div(d, 2 * xdim)
    nxt = lax.rem(d + 1, n)
    prv = lax.rem(d + n - 1, n)

    def leaf_at(zz, xx, cc):
        return (zz * xdim + xx) * 2 + cc

    def rc(src, dst, ssem, rsem, leaf, rhs):
        return pltpu.make_async_remote_copy(
            src_ref=src, dst_ref=dst, send_sem=ssem, recv_sem=rsem,
            device_id=(leaf, rhs), device_id_type=MESH,
        )

    leaves = pts.shape[0]
    leaf_pts = pts.shape[1]
    features = pts.shape[2]
    cols = vt.shape[1]
    rank = bases.shape[2]
    scale = math.log2(math.e) / features

    barrier = pltpu.get_barrier_semaphore()
    partners = [(nxt, r), (prv, r)]
    partners += [(d, lax.rem(r + j, ydim)) for j in range(1, ydim)]
    partners += [(leaf_at(lax.rem(z + s, zdim), x, core), r) for s in range(1, zdim)]
    partners += [(leaf_at(z, lax.rem(x + j, xdim), core), r) for j in range(1, xdim)]
    partners += [(leaf_at(z, x, 1 - core), r)]
    for who in partners:
        pl.semaphore_signal(barrier, inc=1, device_id=who, device_id_type=MESH)

    loads = [
        pltpu.make_async_copy(vt, vall.at[r], lsem.at[0]),
        pltpu.make_async_copy(bases, bv, lsem.at[1]),
        pltpu.make_async_copy(tr, tv, lsem.at[2]),
        pltpu.make_async_copy(pts, pv, lsem.at[3]),
        pltpu.make_async_copy(lc, lv, lsem.at[4]),
        pltpu.make_async_copy(uc, uv, lsem.at[5]),
    ]
    for copy in loads:
        copy.start()

    pl.semaphore_wait(barrier, len(partners))

    half_leaves = leaves // 2
    points_out = [
        rc(pts.at[r], hp.at[0], hp_s.at[0], hp_r.at[0], prv, r),
        rc(pts.at[half_leaves + r], hp.at[1], hp_s.at[1], hp_r.at[1], nxt, r),
    ]
    lists_out = [
        rc(nl, nlr.at[0], nl_s.at[0], nl_r.at[0], prv, r),
        rc(nl, nlr.at[1], nl_s.at[1], nl_r.at[1], nxt, r),
    ]
    vectors_out = [
        rc(vt, vall.at[r], v_s.at[j - 1], v_r.at[j - 1], d, lax.rem(r + j, ydim)) for j in range(1, ydim)
    ]
    for copy in vectors_out + points_out + lists_out:
        copy.start()

    loads[0].wait()
    loads[1].wait()
    loads[2].wait()
    coeffs = []
    for i in range(leaves):
        bh, bl = split(bv[i])
        v = vall[r, i]
        coeffs.append(mm(v, bh) + mm(v, bl))
    parents = []
    for i in range(leaves):
        th, tl = split(tv[i])
        ch, cl = split(coeffs[i])
        lifted = mm(ch, th) + (mm(cl, th) + mm(ch, tl))
        if i % 2 == 0:
            parents.append(lifted)
        else:
            parents[-1] = parents[-1] + lifted
    parts = coeffs + parents
    for m in range(len(parts) // 2):
        gat[z, x, core, m] = jnp.concatenate(parts[2 * m : 2 * m + 2], axis=1).astype(BF16)

    nl_own = nl[...]
    lane = lax.broadcasted_iota(jnp.int32, (leaves, 128), 1) + (d - 1) * leaves

    def mask_of(lists):
        total = jnp.zeros((leaves, 128), F32)
        for k in range(lists.shape[1]):
            entry = lists[:, k : k + 1]
            total = total + jnp.where((entry == lane) & (entry >= 0), 1.0, 0.0).astype(F32)
        return total

    masks[2] = mask_of(nl_own)
    lane_half = lax.broadcasted_iota(jnp.int32, (cols, 128), 1)
    halves[0] = jnp.where(lane_half < rank, 1.0, 0.0).astype(BF16)
    halves[1] = jnp.where(lane_half < rank, 0.0, 1.0).astype(BF16)

    loads[3].wait()

    def norms(index, block):
        wide = block.astype(F32)
        col = jnp.broadcast_to(jnp.sum(wide * wide, axis=1, keepdims=True) * (-scale), (leaf_pts, 128))
        ncol[index] = col
        nrow[index] = jnp.transpose(col)[0:1, :]

    for i in range(leaves):
        norms(i, pv[i])

    order = sorted(range(1, zdim), key=lambda s: (min(s, zdim - s), s))
    z_out = {
        s: rc(
            gat.at[z, x, core], gat.at[z, x, core], z_s.at[s], z_r.at[s],
            leaf_at(lax.rem(z + s, zdim), x, core), r,
        )
        for s in order
    }
    for s in order:
        z_out[s].start()

    x_out = []

    def forward(s):
        zz = lax.rem(z + zdim - s, zdim)
        block = gat.at[zz, x, core]
        if s:
            rc(block, block, z_s.at[s], z_r.at[s], d, r).wait_recv()
        for j in range(1, xdim):
            copy = rc(
                block, block, x_s.at[s, j - 1], x_r.at[s, j - 1],
                leaf_at(z, lax.rem(x + j, xdim), core), r,
            )
            copy.start()
            x_out.append(copy)

    forward(0)
    for i in range(leaves):
        acc[i] = jnp.zeros((ydim, cols, leaf_pts), F32)
    hacc[...] = jnp.zeros((2, ydim * cols, leaf_pts), F32)

    for j in range(1, ydim):
        source = lax.rem(r + ydim - j, ydim)
        rc(vt, vall.at[source], v_s.at[j - 1], v_r.at[j - 1], d, r).wait_recv()
    hv_out = [
        rc(vall.at[:, r], hv.at[0], hv_s.at[0], hv_r.at[0], prv, r),
        rc(vall.at[:, half_leaves + r], hv.at[1], hv_s.at[1], hv_r.at[1], nxt, r),
    ]
    for copy in hv_out:
        copy.start()

    lane1 = lax.broadcasted_iota(jnp.int32, (1, 128), 1)

    def mask_at(which, row, w):
        values = masks[which, pl.ds(row, 1), :]
        return jnp.sum(jnp.where(lane1 == w, values, 0.0), axis=1, keepdims=True).astype(BF16)

    def tile_of(xa, xb, ia, ib):
        cross = mm(xa, xb, NT)
        col = ncol[ia]
        return jnp.exp2(cross * (2.0 * scale) + (jnp.concatenate([col, col], axis=1) + nrow[ib])).astype(BF16)

    wide = (ydim * cols, leaf_pts)

    def add(i, value):
        acc[i] = acc[i] + value.reshape(ydim, cols, leaf_pts)

    def own_pair(t):
        shift = t // 2
        a = 2 * r + t % 2 if t < leaves else r
        b = lax.rem(a + shift, leaves)
        tile = tile_of(pv[a], pv[b], a, b)
        vb = vall[:, b].reshape(wide)
        add(a, mm(vb * mask_at(2, a, leaves + b), tile, NT))
        if shift:
            va = vall[:, a].reshape(wide)
            add(b, mm(va * mask_at(2, b, leaves + a), tile, NN))

    for t in range(leaves + 1):
        own_pair(t)
        if t < zdim - 1:
            forward(order[t])

    c_out = []

    def to_sibling(j):
        column = gat.at[:, lax.rem(x + xdim - j, xdim), core]
        copy = rc(column, column, c_s.at[j], c_r.at[j], leaf_at(z, x, 1 - core), r)
        copy.start()
        c_out.append(copy)

    to_sibling(0)

    for h in range(2):
        points_out[h].wait_recv()
        lists_out[h].wait_recv()
        rc(vall.at[:, r], hv.at[h], hv_s.at[h], hv_r.at[h], d, r).wait_recv()
        masks[h] = mask_of(nlr[h])
        norms(leaves + h, hp[h])

    def halo_pair(p, carry):
        side = lax.div(p + r, leaves)
        o = p + r - half_leaves * side
        tile = tile_of(pv[o], hp[side], o, leaves + side)
        vh = hv[side].reshape(wide)
        add(o, mm(vh * mask_at(2, o, 2 * leaves + r - (leaves + half_leaves) * side), tile, NT))
        vo = vall[:, o].reshape(wide)
        hacc[side] = hacc[side] + mm(vo * mask_at(side, r + half_leaves * side, leaves + o), tile, NN)
        return carry

    for p in range(leaves + 1):
        halo_pair(p, 0)
    hsend[...] = hacc[...].reshape(2, ydim, cols, leaf_pts).astype(BF16)

    loads[4].wait()
    loads[5].wait()

    def widen(dst, src, i):
        for k in range(8):
            w = src[i * 8 + k]
            dst[i, :, 2 * rank * k : 2 * rank * (k + 1)] = jnp.concatenate([w, w], axis=1).astype(BF16)

    widen(wu, uv, 0)
    hs_out = [
        rc(hsend.at[0], hres.at[0], hs_s.at[0], hs_r.at[0], nxt, r),
        rc(hsend.at[1], hres.at[1], hs_s.at[1], hs_r.at[1], prv, r),
    ]
    for copy in hs_out:
        copy.start()
    for q in range(1, leaves // 2):
        widen(wu, uv, q)

    for h in range(2):
        hs_out[h].wait_recv()
        i = r + half_leaves * h
        acc[i] = acc[i] + hres[h].astype(F32)
    for j in range(1, ydim):
        target = lax.rem(r + j, ydim)
        for i in range(leaves):
            asend[j - 1, i] = acc[i, target].astype(BF16)
    widen(wl, lv, 0)
    a_out = [
        rc(asend.at[j - 1], arecv.at[j - 1], a_s.at[j - 1], a_r.at[j - 1], d, lax.rem(r + j, ydim))
        for j in range(1, ydim)
    ]
    for copy in a_out:
        copy.start()
    for i in range(1, leaves):
        widen(wl, lv, i)

    for j in range(1, xdim):
        for s in range(zdim):
            block = gat.at[lax.rem(z + zdim - s, zdim), lax.rem(x + xdim - j, xdim), core]
            rc(block, block, x_s.at[s, j - 1], x_r.at[s, j - 1], d, r).wait_recv()
        to_sibling(j)
    for j in range(ydim - 1):
        a_out[j].wait_recv()
    for j in range(xdim):
        column = gat.at[:, lax.rem(x + xdim - j, xdim), 1 - core]
        rc(column, column, c_s.at[j], c_r.at[j], d, r).wait_recv()

    def gathered(index, per_device, first):
        device = lax.div(index, per_device)
        inner = lax.rem(index, per_device)
        block = gat[
            lax.div(device, 2 * xdim), lax.rem(lax.div(device, 2), xdim), lax.rem(device, 2), first + lax.div(inner, 2)
        ]
        return block * halves[lax.rem(inner, 2)]

    for q in range(leaves // 2):
        left = jnp.concatenate([gathered(fu[q, k], leaves // 2, leaves // 2) for k in range(8)], axis=1)
        upper = mm(left, wu[q], NT)
        uh, ul = split(upper)
        for i in (2 * q, 2 * q + 1):
            left = jnp.concatenate([gathered(fl[i, k], leaves, 0) for k in range(8)], axis=1)
            th, tl = split(tv[i])
            field = mm(left, wl[i], NT) + (mm(uh, th, NT) + mm(ul, th, NT) + mm(uh, tl, NT))
            fh, fo = split(field)
            bh, bl = split(bv[i])
            far = mm(fh, bh, NT) + (mm(fo, bh, NT) + mm(fh, bl, NT))
            near = acc[i, r]
            for j in range(ydim - 1):
                near = near + arecv[j, i].astype(F32)
            out[i] = near + far + RIDGE * vall[r, i].astype(F32)

    for copy in vectors_out + points_out + lists_out + hv_out + hs_out + a_out + x_out + c_out:
        copy.wait_send()
    for s in order:
        z_out[s].wait_send()


def solution(mesh):
    n = mesh.shape["leaf"]
    ydim = mesh.shape["rhs"]
    xdim = 4 if n >= 32 else 2
    zdim = n // (2 * xdim)

    def local(points, vectors, bases, leaf_coupling, transfer, up_coupling, far_leaf, far_up, near_lists):
        leaves, leaf_pts, rank = bases.shape
        cols = vectors.shape[1]
        features = points.shape[1]
        vt = jnp.transpose(vectors.reshape(leaves, leaf_pts, cols), (0, 2, 1))
        anywhere = pl.BlockSpec(memory_space=pl.ANY)
        vmem = pl.BlockSpec(memory_space=pltpu.VMEM)
        smem = pl.BlockSpec(memory_space=pltpu.SMEM)
        dma = pltpu.SemaphoreType.DMA
        wide = ydim * cols
        outT = pl.pallas_call(
            functools.partial(kernel, (zdim, xdim, ydim)),
            out_shape=jax.ShapeDtypeStruct((leaves, cols, leaf_pts), F32),
            in_specs=[anywhere] * 6 + [smem, smem, vmem],
            out_specs=vmem,
            scratch_shapes=[
                pltpu.VMEM((leaves, leaf_pts, features), BF16),
                pltpu.VMEM((2, leaf_pts, features), BF16),
                pltpu.VMEM((ydim, leaves, cols, leaf_pts), BF16),
                pltpu.VMEM((2, ydim, cols, leaf_pts), BF16),
                pltpu.VMEM((2,) + near_lists.shape, jnp.int32),
                pltpu.VMEM((3, leaves, 128), F32),
                pltpu.VMEM(bases.shape, F32),
                pltpu.VMEM((leaves * 8, rank, rank), F32),
                pltpu.VMEM(transfer.shape, F32),
                pltpu.VMEM((leaves * 4, rank, rank), F32),
                pltpu.VMEM((zdim, xdim, 2, leaves * 3 // 4, cols, 2 * rank), BF16),
                pltpu.VMEM((leaves, rank, 16 * rank), BF16),
                pltpu.VMEM((leaves // 2, rank, 16 * rank), BF16),
                pltpu.VMEM((2, cols, 2 * rank), BF16),
                pltpu.VMEM((leaves + 2, leaf_pts, 128), F32),
                pltpu.VMEM((leaves + 2, 1, leaf_pts), F32),
                pltpu.VMEM((leaves, ydim, cols, leaf_pts), F32),
                pltpu.VMEM((2, wide, leaf_pts), F32),
                pltpu.VMEM((2, ydim, cols, leaf_pts), BF16),
                pltpu.VMEM((2, ydim, cols, leaf_pts), BF16),
                pltpu.VMEM((ydim - 1, leaves, cols, leaf_pts), BF16),
                pltpu.VMEM((ydim - 1, leaves, cols, leaf_pts), BF16),
                dma((6,)),
                dma((2,)), dma((2,)),
                dma((ydim - 1,)), dma((ydim - 1,)),
                dma((2,)), dma((2,)),
                dma((2,)), dma((2,)),
                dma((zdim,)), dma((zdim,)),
                dma((zdim, xdim - 1)), dma((zdim, xdim - 1)),
                dma((xdim,)), dma((xdim,)),
                dma((2,)), dma((2,)),
                dma((ydim - 1,)), dma((ydim - 1,)),
            ],
            compiler_params=pltpu.CompilerParams(
                collective_id=0, has_side_effects=True, vmem_limit_bytes=56 * 1024 * 1024
            ),
        )(
            points.reshape(leaves, leaf_pts, features),
            vt,
            bases,
            leaf_coupling.reshape(-1, rank, rank),
            transfer,
            up_coupling.reshape(-1, rank, rank),
            far_leaf,
            far_up,
            near_lists,
        )
        return jnp.transpose(outT, (0, 2, 1)).reshape(leaves * leaf_pts, cols)

    return jax.shard_map(
        local,
        mesh=mesh,
        in_specs=(
            P("leaf", None),
            P("leaf", "rhs"),
            P("leaf", None, None),
            P("leaf", None, None, None),
            P("leaf", None, None),
            P("leaf", None, None, None),
            P("leaf", None),
            P("leaf", None),
            P("leaf", None),
        ),
        out_specs=P("leaf", "rhs"),
        check_vma=False,
    )
```

```python
import functools
import math

import jax
import jax.numpy as jnp
from jax import lax
from jax.experimental import pallas as pl
from jax.experimental.pallas import tpu as pltpu
from jax.sharding import PartitionSpec as P

MESH = pl.DeviceIdType.MESH
F32 = jnp.float32
BF16 = jnp.bfloat16
RIDGE = 0.5
NN = (((1,), (0,)), ((), ()))
NT = (((1,), (1,)), ((), ()))


def mm(a, b, dims=NN):
    return lax.dot_general(a, b, dims, preferred_element_type=F32)


def split(w):
    high = w.astype(BF16)
    return high, (w - high.astype(F32)).astype(BF16)


def kernel(
    dims,
    pts, vt, bases, lc, tr, uc, fl, fu, nl,
    out,
    pt, pv, hp, vall, hv, nlr, masks, bv, lv, tv, uv, gat, wl, wu, halves,
    ncol, nrow, acc, hacc, hsend, hres, asend, arecv,
    lsem, hp_s, hp_r, v_s, v_r, nl_s, nl_r, hv_s, hv_r, z_s, z_r, x_s, x_r, c_s, c_r, hs_s, hs_r, a_s, a_r,
):
    zdim, xdim, ydim = dims
    n = zdim * xdim * 2
    d = lax.axis_index("leaf")
    r = lax.axis_index("rhs")
    core = lax.rem(d, 2)
    x = lax.rem(lax.div(d, 2), xdim)
    z = lax.div(d, 2 * xdim)
    nxt = lax.rem(d + 1, n)
    prv = lax.rem(d + n - 1, n)

    def leaf_at(zz, xx, cc):
        return (zz * xdim + xx) * 2 + cc

    def rc(src, dst, ssem, rsem, leaf, rhs):
        return pltpu.make_async_remote_copy(
            src_ref=src, dst_ref=dst, send_sem=ssem, recv_sem=rsem,
            device_id=(leaf, rhs), device_id_type=MESH,
        )

    leaves, rank, leaf_pts = bases.shape
    features = pts.shape[0]
    cols = vt.shape[0]
    scale = math.log2(math.e) / features

    barrier = pltpu.get_barrier_semaphore()
    partners = [(nxt, r), (prv, r)]
    partners += [(d, lax.rem(r + j, ydim)) for j in range(1, ydim)]
    partners += [(leaf_at(lax.rem(z + s, zdim), x, core), r) for s in range(1, zdim)]
    right, left = lax.rem(x + 1, xdim), lax.rem(x + xdim - 1, xdim)
    across = lax.rem(x + 2, xdim)
    partners += [(leaf_at(z, right, core), r), (leaf_at(z, left, core), r)]
    partners += [(leaf_at(z, x, 1 - core), r)]
    for who in partners:
        pl.semaphore_signal(barrier, inc=1, device_id=who, device_id_type=MESH)

    loads = [
        pltpu.make_async_copy(vt, vall.at[r], lsem.at[0]),
        pltpu.make_async_copy(bases, bv, lsem.at[1]),
        pltpu.make_async_copy(tr, tv, lsem.at[2]),
        pltpu.make_async_copy(pts, pt, lsem.at[3]),
        pltpu.make_async_copy(lc, lv, lsem.at[4]),
        pltpu.make_async_copy(uc, uv, lsem.at[5]),
    ]
    for copy in loads:
        copy.start()

    pl.semaphore_wait(barrier, len(partners))

    def block_of(i):
        return pl.ds(pl.multiple_of(i * leaf_pts, leaf_pts), leaf_pts)

    half_leaves = leaves // 2
    points_out = [
        rc(pts.at[:, block_of(r)], hp.at[0], hp_s.at[0], hp_r.at[0], prv, r),
        rc(pts.at[:, block_of(half_leaves + r)], hp.at[1], hp_s.at[1], hp_r.at[1], nxt, r),
    ]
    lists_out = [
        rc(nl, nlr.at[0], nl_s.at[0], nl_r.at[0], prv, r),
        rc(nl, nlr.at[1], nl_s.at[1], nl_r.at[1], nxt, r),
    ]
    vectors_out = [
        rc(vt, vall.at[r], v_s.at[j - 1], v_r.at[j - 1], d, lax.rem(r + j, ydim)) for j in range(1, ydim)
    ]
    for copy in vectors_out + points_out + lists_out:
        copy.start()

    loads[0].wait()
    loads[1].wait()
    loads[2].wait()
    coeffs = []
    for i in range(leaves):
        bh, bl = split(bv[i])
        v = vall[r, :, block_of(i)]
        coeffs.append(mm(v, bh, NT) + mm(v, bl, NT))
    parents = []
    for i in range(leaves):
        th, tl = split(tv[i])
        ch, cl = split(coeffs[i])
        lifted = mm(ch, th) + (mm(cl, th) + mm(ch, tl))
        if i % 2 == 0:
            parents.append(lifted)
        else:
            parents[-1] = parents[-1] + lifted
    parts = coeffs + parents
    for m in range(len(parts) // 2):
        gat[z, x, core, m] = jnp.concatenate(parts[2 * m : 2 * m + 2], axis=1).astype(BF16)

    nl_own = nl[...]
    lane = lax.broadcasted_iota(jnp.int32, (leaves, 128), 1) + (d - 1) * leaves

    def mask_of(lists):
        total = jnp.zeros((leaves, 128), F32)
        for k in range(lists.shape[1]):
            entry = lists[:, k : k + 1]
            total = total + jnp.where((entry == lane) & (entry >= 0), 1.0, 0.0).astype(F32)
        return total

    masks[2] = mask_of(nl_own)
    lane_half = lax.broadcasted_iota(jnp.int32, (cols, 128), 1)
    halves[0] = jnp.where(lane_half < rank, 1.0, 0.0).astype(BF16)
    halves[1] = jnp.where(lane_half < rank, 0.0, 1.0).astype(BF16)

    loads[3].wait()

    def norms(index, block):
        wide = block.astype(F32)
        row = jnp.sum(wide * wide, axis=0, keepdims=True) * (-scale)
        nrow[index] = row
        if index < leaves:
            ncol[index] = jnp.transpose(jnp.broadcast_to(row, (128, leaf_pts)))

    for i in range(leaves):
        norms(i, pt[:, block_of(i)])

    order = sorted(range(1, zdim), key=lambda s: (min(s, zdim - s), s))
    z_out = {
        s: rc(
            gat.at[z, x, core], gat.at[z, x, core], z_s.at[s], z_r.at[s],
            leaf_at(lax.rem(z + s, zdim), x, core), r,
        )
        for s in order
    }
    for s in order:
        z_out[s].start()

    x_out = []
    steps = [0] + order

    def x_send(s, column, kind, target):
        block = gat.at[lax.rem(z + zdim - s, zdim), column, core]
        copy = rc(block, block, x_s.at[s, kind], x_r.at[s, kind], leaf_at(z, target, core), r)
        copy.start()
        x_out.append(copy)

    def x_wait(s, column, kind):
        block = gat.at[lax.rem(z + zdim - s, zdim), column, core]
        rc(block, block, x_s.at[s, kind], x_r.at[s, kind], d, r).wait_recv()

    def forward(s):
        if s:
            block = gat.at[lax.rem(z + zdim - s, zdim), x, core]
            rc(block, block, z_s.at[s], z_r.at[s], d, r).wait_recv()
        x_send(s, x, 0, right)
        x_send(s, x, 1, left)

    def relay(m):
        s = steps[m]
        if m % 2 == 0:
            x_wait(s, left, 0)
            x_send(s, left, 2, right)
        else:
            x_wait(s, right, 1)
            x_send(s, right, 2, left)

    forward(0)
    for i in range(leaves):
        acc[i] = jnp.zeros((ydim, cols, leaf_pts), F32)
    hacc[...] = jnp.zeros((2, ydim * cols, leaf_pts), F32)

    for j in range(1, ydim):
        source = lax.rem(r + ydim - j, ydim)
        rc(vt, vall.at[source], v_s.at[j - 1], v_r.at[j - 1], d, r).wait_recv()
    hv_out = [
        rc(vall.at[:, :, block_of(r)], hv.at[0], hv_s.at[0], hv_r.at[0], prv, r),
        rc(vall.at[:, :, block_of(half_leaves + r)], hv.at[1], hv_s.at[1], hv_r.at[1], nxt, r),
    ]
    for copy in hv_out:
        copy.start()

    lane1 = lax.broadcasted_iota(jnp.int32, (1, 128), 1)

    def mask_at(which, row, w):
        values = masks[which, pl.ds(row, 1), :]
        return jnp.sum(jnp.where(lane1 == w, values, 0.0), axis=1, keepdims=True).astype(BF16)

    def tile_of(xa, xb, ia, ib):
        cross = mm(xa, xb)
        col = ncol[ia]
        return jnp.exp2(cross * (2.0 * scale) + (jnp.concatenate([col, col], axis=1) + nrow[ib])).astype(BF16)

    wide = (ydim * cols, leaf_pts)

    def add(i, value):
        acc[i] = acc[i] + value.reshape(ydim, cols, leaf_pts)

    def own_pair(t):
        shift = t // 2
        a = 2 * r + t % 2 if t < leaves else r
        b = lax.rem(a + shift, leaves)
        tile = tile_of(pv[a], pt[:, block_of(b)], a, b)
        vb = vall[:, :, block_of(b)].reshape(wide)
        add(a, mm(vb * mask_at(2, a, leaves + b), tile, NT))
        if shift:
            va = vall[:, :, block_of(a)].reshape(wide)
            add(b, mm(va * mask_at(2, b, leaves + a), tile, NN))

    for i in range(leaves):
        pv[i] = jnp.transpose(pt[:, block_of(i)])
    for t in range(leaves + 1):
        own_pair(t)
        if t < zdim - 1:
            forward(order[t])
        if t >= 3:
            relay(t - 3)

    c_out = []

    def to_sibling(m, j):
        column = gat.at[:, j, core]
        copy = rc(column, column, c_s.at[m], c_r.at[m], leaf_at(z, x, 1 - core), r)
        copy.start()
        c_out.append(copy)

    to_sibling(0, x)

    for h in range(2):
        points_out[h].wait_recv()
        lists_out[h].wait_recv()
        rc(vall.at[:, :, block_of(r)], hv.at[h], hv_s.at[h], hv_r.at[h], d, r).wait_recv()
        masks[h] = mask_of(nlr[h])
        norms(leaves + h, hp[h])

    def halo_pair(p, carry):
        side = lax.div(p + r, leaves)
        o = p + r - half_leaves * side
        tile = tile_of(pv[o], hp[side], o, leaves + side)
        vh = hv[side].reshape(wide)
        add(o, mm(vh * mask_at(2, o, 2 * leaves + r - (leaves + half_leaves) * side), tile, NT))
        vo = vall[:, :, block_of(o)].reshape(wide)
        hacc[side] = hacc[side] + mm(vo * mask_at(side, r + half_leaves * side, leaves + o), tile, NN)
        return carry

    for p in range(leaves + 1):
        halo_pair(p, 0)
        if p < 2:
            relay(6 + p)
    hsend[...] = hacc[...].reshape(2, ydim, cols, leaf_pts).astype(BF16)

    loads[4].wait()
    loads[5].wait()

    def widen(dst, src, i):
        for k in range(8):
            w = src[i * 8 + k]
            dst[i, :, 2 * rank * k : 2 * rank * (k + 1)] = jnp.concatenate([w, w], axis=1).astype(BF16)

    widen(wu, uv, 0)
    hs_out = [
        rc(hsend.at[0], hres.at[0], hs_s.at[0], hs_r.at[0], nxt, r),
        rc(hsend.at[1], hres.at[1], hs_s.at[1], hs_r.at[1], prv, r),
    ]
    for copy in hs_out:
        copy.start()
    for q in range(1, leaves // 2):
        widen(wu, uv, q)

    for h in range(2):
        hs_out[h].wait_recv()
        i = r + half_leaves * h
        acc[i] = acc[i] + hres[h].astype(F32)
    for j in range(1, ydim):
        target = lax.rem(r + j, ydim)
        for i in range(leaves):
            asend[j - 1, i] = acc[i, target].astype(BF16)
    widen(wl, lv, 0)
    a_out = [
        rc(asend.at[j - 1], arecv.at[j - 1], a_s.at[j - 1], a_r.at[j - 1], d, lax.rem(r + j, ydim))
        for j in range(1, ydim)
    ]
    for copy in a_out:
        copy.start()
    for i in range(1, leaves):
        widen(wl, lv, i)

    for m in range(1, zdim, 2):
        x_wait(steps[m], left, 0)
    to_sibling(1, left)
    for m in range(0, zdim, 2):
        x_wait(steps[m], right, 1)
    to_sibling(2, right)
    for m in range(zdim):
        x_wait(steps[m], across, 2)
    to_sibling(3, across)
    for j in range(ydim - 1):
        a_out[j].wait_recv()
    for m, j in enumerate((x, left, right, across)):
        column = gat.at[:, j, 1 - core]
        rc(column, column, c_s.at[m], c_r.at[m], d, r).wait_recv()

    def gathered(index, per_device, first):
        device = lax.div(index, per_device)
        inner = lax.rem(index, per_device)
        block = gat[
            lax.div(device, 2 * xdim), lax.rem(lax.div(device, 2), xdim), lax.rem(device, 2), first + lax.div(inner, 2)
        ]
        return block * halves[lax.rem(inner, 2)]

    for q in range(leaves // 2):
        left = jnp.concatenate([gathered(fu[q, k], leaves // 2, leaves // 2) for k in range(8)], axis=1)
        upper = mm(left, wu[q], NT)
        uh, ul = split(upper)
        for i in (2 * q, 2 * q + 1):
            left = jnp.concatenate([gathered(fl[i, k], leaves, 0) for k in range(8)], axis=1)
            th, tl = split(tv[i])
            field = mm(left, wl[i], NT) + (mm(uh, th, NT) + mm(ul, th, NT) + mm(uh, tl, NT))
            fh, fo = split(field)
            bh, bl = split(bv[i])
            far = mm(fh, bh) + (mm(fo, bh) + mm(fh, bl))
            near = acc[i, r]
            for j in range(ydim - 1):
                near = near + arecv[j, i].astype(F32)
            out[:, block_of(i)] = near + far + RIDGE * vall[r, :, block_of(i)].astype(F32)

    for copy in vectors_out + points_out + lists_out + hv_out + hs_out + a_out + x_out + c_out:
        copy.wait_send()
    for s in order:
        z_out[s].wait_send()


def solution(mesh):
    n = mesh.shape["leaf"]
    ydim = mesh.shape["rhs"]
    xdim = 4 if n >= 32 else 2
    zdim = n // (2 * xdim)

    def local(points, vectors, bases, leaf_coupling, transfer, up_coupling, far_leaf, far_up, near_lists):
        leaves, leaf_pts, rank = bases.shape
        cols = vectors.shape[1]
        features = points.shape[1]
        anywhere = pl.BlockSpec(memory_space=pl.ANY)
        vmem = pl.BlockSpec(memory_space=pltpu.VMEM)
        smem = pl.BlockSpec(memory_space=pltpu.SMEM)
        dma = pltpu.SemaphoreType.DMA
        wide = ydim * cols
        outT = pl.pallas_call(
            functools.partial(kernel, (zdim, xdim, ydim)),
            out_shape=jax.ShapeDtypeStruct((cols, leaves * leaf_pts), F32),
            in_specs=[anywhere] * 6 + [smem, smem, vmem],
            out_specs=vmem,
            scratch_shapes=[
                pltpu.VMEM((features, leaves * leaf_pts), BF16),
                pltpu.VMEM((leaves, leaf_pts, features), BF16),
                pltpu.VMEM((2, features, leaf_pts), BF16),
                pltpu.VMEM((ydim, cols, leaves * leaf_pts), BF16),
                pltpu.VMEM((2, ydim, cols, leaf_pts), BF16),
                pltpu.VMEM((2,) + near_lists.shape, jnp.int32),
                pltpu.VMEM((3, leaves, 128), F32),
                pltpu.VMEM((leaves, rank, leaf_pts), F32),
                pltpu.VMEM((leaves * 8, rank, rank), F32),
                pltpu.VMEM(transfer.shape, F32),
                pltpu.VMEM((leaves * 4, rank, rank), F32),
                pltpu.VMEM((zdim, xdim, 2, leaves * 3 // 4, cols, 2 * rank), BF16),
                pltpu.VMEM((leaves, rank, 16 * rank), BF16),
                pltpu.VMEM((leaves // 2, rank, 16 * rank), BF16),
                pltpu.VMEM((2, cols, 2 * rank), BF16),
                pltpu.VMEM((leaves + 2, leaf_pts, 128), F32),
                pltpu.VMEM((leaves + 2, 1, leaf_pts), F32),
                pltpu.VMEM((leaves, ydim, cols, leaf_pts), F32),
                pltpu.VMEM((2, wide, leaf_pts), F32),
                pltpu.VMEM((2, ydim, cols, leaf_pts), BF16),
                pltpu.VMEM((2, ydim, cols, leaf_pts), BF16),
                pltpu.VMEM((ydim - 1, leaves, cols, leaf_pts), BF16),
                pltpu.VMEM((ydim - 1, leaves, cols, leaf_pts), BF16),
                dma((6,)),
                dma((2,)), dma((2,)),
                dma((ydim - 1,)), dma((ydim - 1,)),
                dma((2,)), dma((2,)),
                dma((2,)), dma((2,)),
                dma((zdim,)), dma((zdim,)),
                dma((zdim, 3)), dma((zdim, 3)),
                dma((xdim,)), dma((xdim,)),
                dma((2,)), dma((2,)),
                dma((ydim - 1,)), dma((ydim - 1,)),
            ],
            compiler_params=pltpu.CompilerParams(
                collective_id=0, has_side_effects=True, vmem_limit_bytes=56 * 1024 * 1024
            ),
        )(
            points.T,
            vectors.T,
            jnp.transpose(bases, (0, 2, 1)),
            leaf_coupling.reshape(-1, rank, rank),
            transfer,
            up_coupling.reshape(-1, rank, rank),
            far_leaf,
            far_up,
            near_lists,
        )
        return outT.T

    return jax.shard_map(
        local,
        mesh=mesh,
        in_specs=(
            P("leaf", None),
            P("leaf", "rhs"),
            P("leaf", None, None),
            P("leaf", None, None, None),
            P("leaf", None, None),
            P("leaf", None, None, None),
            P("leaf", None),
            P("leaf", None),
            P("leaf", None),
        ),
        out_specs=P("leaf", "rhs"),
        check_vma=False,
    )
```

```python
import functools
import math

import jax
import jax.numpy as jnp
from jax import lax
from jax.experimental import pallas as pl
from jax.experimental.pallas import tpu as pltpu
from jax.sharding import PartitionSpec as P

MESH = pl.DeviceIdType.MESH
F32 = jnp.float32
BF16 = jnp.bfloat16
RIDGE = 0.5
NN = (((1,), (0,)), ((), ()))
NT = (((1,), (1,)), ((), ()))


def mm(a, b, dims=NN):
    return lax.dot_general(a, b, dims, preferred_element_type=F32)


def split(w):
    high = w.astype(BF16)
    return high, (w - high.astype(F32)).astype(BF16)


def kernel(
    dims,
    pts, vt, bases, lc, tr, uc, fl, fu, nl,
    out,
    pt, pv, hp, vall, hv, nlr, masks, bv, lv, tv, uv, gat, wl, wu, halves,
    ncol, nrow, tiles, acc, hacc, hsend, hres, asend, arecv,
    lsem, hp_s, hp_r, v_s, v_r, nl_s, nl_r, hv_s, hv_r, z_s, z_r, x_s, x_r, c_s, c_r, hs_s, hs_r, a_s, a_r,
):
    zdim, xdim, ydim = dims
    n = zdim * xdim * 2
    d = lax.axis_index("leaf")
    r = lax.axis_index("rhs")
    core = lax.rem(d, 2)
    x = lax.rem(lax.div(d, 2), xdim)
    z = lax.div(d, 2 * xdim)
    nxt = lax.rem(d + 1, n)
    prv = lax.rem(d + n - 1, n)

    def leaf_at(zz, xx, cc):
        return (zz * xdim + xx) * 2 + cc

    def rc(src, dst, ssem, rsem, leaf, rhs):
        return pltpu.make_async_remote_copy(
            src_ref=src, dst_ref=dst, send_sem=ssem, recv_sem=rsem,
            device_id=(leaf, rhs), device_id_type=MESH,
        )

    leaves, rank, leaf_pts = bases.shape
    features = pts.shape[0]
    cols = vt.shape[0]
    scale = math.log2(math.e) / features

    barrier = pltpu.get_barrier_semaphore()
    rhs_at = [lax.rem(r + j, ydim) for j in range(ydim)]
    rhs_from = [lax.rem(r + ydim - j, ydim) for j in range(ydim)]
    partners = [(side, to) for side in (nxt, prv) for to in rhs_at]
    partners += [(d, to) for to in rhs_at[1:]]
    partners += [(leaf_at(lax.rem(z + s, zdim), x, core), r) for s in range(1, zdim)]
    right, left = lax.rem(x + 1, xdim), lax.rem(x + xdim - 1, xdim)
    across = lax.rem(x + 2, xdim)
    partners += [(leaf_at(z, right, core), r), (leaf_at(z, left, core), r)]
    partners += [(leaf_at(z, x, 1 - core), r)]
    for who in partners:
        pl.semaphore_signal(barrier, inc=1, device_id=who, device_id_type=MESH)

    loads = [
        pltpu.make_async_copy(vt, vall.at[r], lsem.at[0]),
        pltpu.make_async_copy(bases, bv, lsem.at[1]),
        pltpu.make_async_copy(tr, tv, lsem.at[2]),
        pltpu.make_async_copy(pts, pt, lsem.at[3]),
        pltpu.make_async_copy(lc, lv, lsem.at[4]),
        pltpu.make_async_copy(uc, uv, lsem.at[5]),
    ]
    for copy in loads:
        copy.start()

    pl.semaphore_wait(barrier, len(partners))

    def block_of(i):
        return pl.ds(pl.multiple_of(i * leaf_pts, leaf_pts), leaf_pts)

    half_leaves = leaves // 2
    points_out = [
        rc(pts.at[:, block_of(r)], hp.at[0], hp_s.at[0], hp_r.at[0], prv, r),
        rc(pts.at[:, block_of(half_leaves + r)], hp.at[1], hp_s.at[1], hp_r.at[1], nxt, r),
    ]
    lists_out = [
        rc(nl, nlr.at[0], nl_s.at[0], nl_r.at[0], prv, r),
        rc(nl, nlr.at[1], nl_s.at[1], nl_r.at[1], nxt, r),
    ]
    vectors_out = [
        rc(vt, vall.at[r], v_s.at[j - 1], v_r.at[j - 1], d, rhs_at[j]) for j in range(1, ydim)
    ]
    hv_out = []
    for j in range(ydim):
        to = rhs_at[j]
        hv_out += [
            rc(vt.at[:, block_of(to)], hv.at[0, r], hv_s.at[0, j], hv_r.at[0, j], prv, to),
            rc(vt.at[:, block_of(half_leaves + to)], hv.at[1, r], hv_s.at[1, j], hv_r.at[1, j], nxt, to),
        ]
    for copy in vectors_out + points_out + hv_out + lists_out:
        copy.start()

    loads[0].wait()
    loads[1].wait()
    loads[2].wait()
    coeffs = []
    for i in range(leaves):
        bh, bl = split(bv[i])
        v = vall[r, :, block_of(i)]
        coeffs.append(mm(v, bh, NT) + mm(v, bl, NT))
    parents = []
    for i in range(leaves):
        th, tl = split(tv[i])
        ch, cl = split(coeffs[i])
        lifted = mm(ch, th) + (mm(cl, th) + mm(ch, tl))
        if i % 2 == 0:
            parents.append(lifted)
        else:
            parents[-1] = parents[-1] + lifted
    parts = coeffs + parents
    for m in range(len(parts) // 2):
        gat[z, x, core, m] = jnp.concatenate(parts[2 * m : 2 * m + 2], axis=1).astype(BF16)

    nl_own = nl[...]
    lane = lax.broadcasted_iota(jnp.int32, (leaves, 128), 1) + (d - 1) * leaves

    def mask_of(lists):
        total = jnp.zeros((leaves, 128), F32)
        for k in range(lists.shape[1]):
            entry = lists[:, k : k + 1]
            total = total + jnp.where((entry == lane) & (entry >= 0), 1.0, 0.0).astype(F32)
        return total

    masks[2] = mask_of(nl_own)
    lane_half = lax.broadcasted_iota(jnp.int32, (cols, 128), 1)
    halves[0] = jnp.where(lane_half < rank, 1.0, 0.0).astype(BF16)
    halves[1] = jnp.where(lane_half < rank, 0.0, 1.0).astype(BF16)

    loads[3].wait()

    def norms(index, block):
        wide = block.astype(F32)
        row = jnp.sum(wide * wide, axis=0, keepdims=True) * (-scale)
        nrow[index] = row
        if index < leaves:
            ncol[index] = jnp.transpose(jnp.broadcast_to(row, (128, leaf_pts)))

    for i in range(leaves):
        norms(i, pt[:, block_of(i)])

    order = sorted(range(1, zdim), key=lambda s: (min(s, zdim - s), s))
    z_out = {
        s: rc(
            gat.at[z, x, core], gat.at[z, x, core], z_s.at[s], z_r.at[s],
            leaf_at(lax.rem(z + s, zdim), x, core), r,
        )
        for s in order
    }
    for s in order:
        z_out[s].start()

    x_out = []
    steps = [0] + order

    def x_send(s, column, kind, target):
        block = gat.at[lax.rem(z + zdim - s, zdim), column, core]
        copy = rc(block, block, x_s.at[s, kind], x_r.at[s, kind], leaf_at(z, target, core), r)
        copy.start()
        x_out.append(copy)

    def x_wait(s, column, kind):
        block = gat.at[lax.rem(z + zdim - s, zdim), column, core]
        rc(block, block, x_s.at[s, kind], x_r.at[s, kind], d, r).wait_recv()

    def forward(s):
        if s:
            block = gat.at[lax.rem(z + zdim - s, zdim), x, core]
            rc(block, block, z_s.at[s], z_r.at[s], d, r).wait_recv()
        x_send(s, x, 0, right)
        x_send(s, x, 1, left)
        to_sibling(s, x, 3)

    c_out = []

    def to_sibling(s, column, kind):
        block = gat.at[lax.rem(z + zdim - s, zdim), column, core]
        copy = rc(block, block, c_s.at[s, kind], c_r.at[s, kind], leaf_at(z, x, 1 - core), r)
        copy.start()
        c_out.append(copy)

    def relay(m):
        s = steps[m]
        if m % 2 == 0:
            x_wait(s, left, 0)
            x_send(s, left, 2, right)
            to_sibling(s, left, 0)
        else:
            x_wait(s, right, 1)
            x_send(s, right, 2, left)
            to_sibling(s, right, 1)

    forward(0)
    for i in range(leaves):
        acc[i] = jnp.zeros((ydim, cols, leaf_pts), F32)
    hacc[...] = jnp.zeros((2, ydim * cols, leaf_pts), F32)

    lane1 = lax.broadcasted_iota(jnp.int32, (1, 128), 1)

    def mask_at(which, row, w):
        values = masks[which, pl.ds(row, 1), :]
        return jnp.sum(jnp.where(lane1 == w, values, 0.0), axis=1, keepdims=True).astype(BF16)

    def tile_of(xa, xb, ia, ib):
        cross = mm(xa, xb)
        col = ncol[ia]
        return jnp.exp2(cross * (2.0 * scale) + (jnp.concatenate([col, col], axis=1) + nrow[ib])).astype(BF16)

    wide = (ydim * cols, leaf_pts)

    def add(i, value):
        acc[i] = acc[i] + value.reshape(ydim, cols, leaf_pts)

    def pair(t):
        a = 2 * r + t % 2 if t < leaves else r
        return a, lax.rem(a + t // 2, leaves)

    def own_tile(t):
        a, b = pair(t)
        tiles[t] = tile_of(pv[a], pt[:, block_of(b)], a, b)

    def own_products(t):
        a, b = pair(t)
        vb = vall[:, :, block_of(b)].reshape(wide)
        add(a, mm(vb * mask_at(2, a, leaves + b), tiles[t], NT))
        if t // 2:
            va = vall[:, :, block_of(a)].reshape(wide)
            add(b, mm(va * mask_at(2, b, leaves + a), tiles[t], NN))

    for i in range(leaves):
        pv[i] = jnp.transpose(pt[:, block_of(i)])
    at = {(0, 4): 0, (0, 6): 1, (0, 8): 2, (1, 1): 3, (1, 3): 4, (1, 5): 5, (1, 7): 6}
    for t in range(leaves + 1):
        own_tile(t)
        if (0, t) in at:
            forward(order[at[0, t]])
    for j in range(1, ydim):
        rc(vt, vall.at[rhs_from[j]], v_s.at[j - 1], v_r.at[j - 1], d, r).wait_recv()
    for t in range(leaves + 1):
        own_products(t)
        if (1, t) in at:
            forward(order[at[1, t]])
        if t == leaves:
            relay(0)

    for h in range(2):
        points_out[h].wait_recv()
        lists_out[h].wait_recv()
        for j in range(ydim):
            rc(vt.at[:, block_of(r)], hv.at[h, rhs_from[j]], hv_s.at[h, j], hv_r.at[h, j], d, r).wait_recv()
        masks[h] = mask_of(nlr[h])
        norms(leaves + h, hp[h])

    def halo_pair(p, carry):
        side = lax.div(p + r, leaves)
        o = p + r - half_leaves * side
        tile = tile_of(pv[o], hp[side], o, leaves + side)
        vh = hv[side].reshape(wide)
        add(o, mm(vh * mask_at(2, o, 2 * leaves + r - (leaves + half_leaves) * side), tile, NT))
        vo = vall[:, :, block_of(o)].reshape(wide)
        hacc[side] = hacc[side] + mm(vo * mask_at(side, r + half_leaves * side, leaves + o), tile, NN)
        return carry

    for p in range(leaves + 1):
        halo_pair(p, 0)
        if p in (2, 5, 8):
            relay(1 + p // 3)
    hsend[...] = hacc[...].reshape(2, ydim, cols, leaf_pts).astype(BF16)

    for j in (2, 1, 3):
        for i in range(leaves):
            asend[j - 1, i] = acc[i, rhs_at[j]].astype(BF16)

    loads[4].wait()
    loads[5].wait()

    def widen(dst, src, i):
        for k in range(8):
            w = src[i * 8 + k]
            dst[i, :, 2 * rank * k : 2 * rank * (k + 1)] = jnp.concatenate([w, w], axis=1).astype(BF16)

    widen(wu, uv, 0)
    a_out = [
        rc(asend.at[j - 1], arecv.at[j - 1], a_s.at[j - 1], a_r.at[j - 1], d, rhs_at[j]) for j in (2, 1, 3)
    ]
    hs_out = []
    for j in range(ydim):
        to = rhs_at[j]
        hs_out += [
            rc(hsend.at[0, to], hres.at[0, r], hs_s.at[0, j], hs_r.at[0, j], nxt, to),
            rc(hsend.at[1, to], hres.at[1, r], hs_s.at[1, j], hs_r.at[1, j], prv, to),
        ]
    for copy in a_out + hs_out:
        copy.start()
    relay(4)
    for q in range(1, leaves // 2):
        widen(wu, uv, q)
    relay(5)
    for i in range(leaves // 2):
        widen(wl, lv, i)
    relay(6)
    for i in range(leaves // 2, leaves):
        widen(wl, lv, i)
    relay(7)

    for m in range(zdim):
        if m % 2:
            x_wait(steps[m], left, 0)
            to_sibling(steps[m], left, 0)
        else:
            x_wait(steps[m], right, 1)
            to_sibling(steps[m], right, 1)
        x_wait(steps[m], across, 2)
        to_sibling(steps[m], across, 2)
    for j in range(ydim - 1):
        a_out[j].wait_recv()
    for h in range(2):
        for j in range(ydim):
            rc(hsend.at[h, r], hres.at[h, rhs_from[j]], hs_s.at[h, j], hs_r.at[h, j], d, r).wait_recv()
    for s in steps:
        for kind, column in enumerate((left, right, across, x)):
            block = gat.at[lax.rem(z + zdim - s, zdim), column, 1 - core]
            rc(block, block, c_s.at[s, kind], c_r.at[s, kind], d, r).wait_recv()

    def gathered(index, per_device, first):
        device = lax.div(index, per_device)
        inner = lax.rem(index, per_device)
        block = gat[
            lax.div(device, 2 * xdim), lax.rem(lax.div(device, 2), xdim), lax.rem(device, 2), first + lax.div(inner, 2)
        ]
        return block * halves[lax.rem(inner, 2)]

    for q in range(leaves // 2):
        left = jnp.concatenate([gathered(fu[q, k], leaves // 2, leaves // 2) for k in range(8)], axis=1)
        upper = mm(left, wu[q], NT)
        uh, ul = split(upper)
        for i in (2 * q, 2 * q + 1):
            left = jnp.concatenate([gathered(fl[i, k], leaves, 0) for k in range(8)], axis=1)
            th, tl = split(tv[i])
            field = mm(left, wl[i], NT) + (mm(uh, th, NT) + mm(ul, th, NT) + mm(uh, tl, NT))
            fh, fo = split(field)
            bh, bl = split(bv[i])
            far = mm(fh, bh) + (mm(fo, bh) + mm(fh, bl))
            near = acc[i, r] + hres[i // half_leaves, i % half_leaves].astype(F32)
            for j in range(ydim - 1):
                near = near + arecv[j, i].astype(F32)
            out[:, block_of(i)] = near + far + RIDGE * vall[r, :, block_of(i)].astype(F32)

    for copy in vectors_out + points_out + lists_out + hv_out + hs_out + a_out + x_out + c_out:
        copy.wait_send()
    for s in order:
        z_out[s].wait_send()


def solution(mesh):
    n = mesh.shape["leaf"]
    ydim = mesh.shape["rhs"]
    xdim = 4 if n >= 32 else 2
    zdim = n // (2 * xdim)

    def local(points, vectors, bases, leaf_coupling, transfer, up_coupling, far_leaf, far_up, near_lists):
        leaves, leaf_pts, rank = bases.shape
        cols = vectors.shape[1]
        features = points.shape[1]
        anywhere = pl.BlockSpec(memory_space=pl.ANY)
        vmem = pl.BlockSpec(memory_space=pltpu.VMEM)
        smem = pl.BlockSpec(memory_space=pltpu.SMEM)
        dma = pltpu.SemaphoreType.DMA
        wide = ydim * cols
        outT = pl.pallas_call(
            functools.partial(kernel, (zdim, xdim, ydim)),
            out_shape=jax.ShapeDtypeStruct((cols, leaves * leaf_pts), F32),
            in_specs=[anywhere] * 6 + [smem, smem, vmem],
            out_specs=vmem,
            scratch_shapes=[
                pltpu.VMEM((features, leaves * leaf_pts), BF16),
                pltpu.VMEM((leaves, leaf_pts, features), BF16),
                pltpu.VMEM((2, features, leaf_pts), BF16),
                pltpu.VMEM((ydim, cols, leaves * leaf_pts), BF16),
                pltpu.VMEM((2, ydim, cols, leaf_pts), BF16),
                pltpu.VMEM((2,) + near_lists.shape, jnp.int32),
                pltpu.VMEM((3, leaves, 128), F32),
                pltpu.VMEM((leaves, rank, leaf_pts), F32),
                pltpu.VMEM((leaves * 8, rank, rank), F32),
                pltpu.VMEM(transfer.shape, F32),
                pltpu.VMEM((leaves * 4, rank, rank), F32),
                pltpu.VMEM((zdim, xdim, 2, leaves * 3 // 4, cols, 2 * rank), BF16),
                pltpu.VMEM((leaves, rank, 16 * rank), BF16),
                pltpu.VMEM((leaves // 2, rank, 16 * rank), BF16),
                pltpu.VMEM((2, cols, 2 * rank), BF16),
                pltpu.VMEM((leaves + 2, leaf_pts, 128), F32),
                pltpu.VMEM((leaves + 2, 1, leaf_pts), F32),
                pltpu.VMEM((leaves + 1, leaf_pts, leaf_pts), BF16),
                pltpu.VMEM((leaves, ydim, cols, leaf_pts), F32),
                pltpu.VMEM((2, wide, leaf_pts), F32),
                pltpu.VMEM((2, ydim, cols, leaf_pts), BF16),
                pltpu.VMEM((2, ydim, cols, leaf_pts), BF16),
                pltpu.VMEM((ydim - 1, leaves, cols, leaf_pts), BF16),
                pltpu.VMEM((ydim - 1, leaves, cols, leaf_pts), BF16),
                dma((6,)),
                dma((2,)), dma((2,)),
                dma((ydim - 1,)), dma((ydim - 1,)),
                dma((2,)), dma((2,)),
                dma((2, ydim)), dma((2, ydim)),
                dma((zdim,)), dma((zdim,)),
                dma((zdim, 3)), dma((zdim, 3)),
                dma((zdim, 4)), dma((zdim, 4)),
                dma((2, ydim)), dma((2, ydim)),
                dma((ydim - 1,)), dma((ydim - 1,)),
            ],
            compiler_params=pltpu.CompilerParams(
                collective_id=0, has_side_effects=True, vmem_limit_bytes=56 * 1024 * 1024
            ),
        )(
            points.T,
            vectors.T,
            jnp.transpose(bases, (0, 2, 1)),
            leaf_coupling.reshape(-1, rank, rank),
            transfer,
            up_coupling.reshape(-1, rank, rank),
            far_leaf,
            far_up,
            near_lists,
        )
        return outT.T

    return jax.shard_map(
        local,
        mesh=mesh,
        in_specs=(
            P("leaf", None),
            P("leaf", "rhs"),
            P("leaf", None, None),
            P("leaf", None, None, None),
            P("leaf", None, None),
            P("leaf", None, None, None),
            P("leaf", None),
            P("leaf", None),
            P("leaf", None),
        ),
        out_specs=P("leaf", "rhs"),
        check_vma=False,
    )
```

```python
import functools
import math

import jax
import jax.numpy as jnp
from jax import lax
from jax.experimental import pallas as pl
from jax.experimental.pallas import tpu as pltpu
from jax.sharding import PartitionSpec as P

MESH = pl.DeviceIdType.MESH
F32 = jnp.float32
BF16 = jnp.bfloat16
RIDGE = 0.5
NN = (((1,), (0,)), ((), ()))
NT = (((1,), (1,)), ((), ()))


def mm(a, b, dims=NN):
    return lax.dot_general(a, b, dims, preferred_element_type=F32)


def split(w):
    high = w.astype(BF16)
    return high, (w - high.astype(F32)).astype(BF16)


def kernel(
    dims,
    pts, vt, bases, lc, tr, uc, fl, fu, nl,
    out,
    pt, pv, hp, vall, hv, nlr, masks, bv, lv, tv, uv, gat, wl, wu, halves,
    ncol, nrow, tiles, acc, hacc, hsend, hres, asend, arecv,
    lsem, hp_s, hp_r, v_s, v_r, nl_s, nl_r, hv_s, hv_r, z_s, z_r, x_s, x_r, c_s, c_r, hs_s, hs_r, a_s, a_r,
):
    zdim, xdim, ydim = dims
    n = zdim * xdim * 2
    d = lax.axis_index("leaf")
    r = lax.axis_index("rhs")
    core = lax.rem(d, 2)
    x = lax.rem(lax.div(d, 2), xdim)
    z = lax.div(d, 2 * xdim)
    nxt = lax.rem(d + 1, n)
    prv = lax.rem(d + n - 1, n)

    def leaf_at(zz, xx, cc):
        return (zz * xdim + xx) * 2 + cc

    def rc(src, dst, ssem, rsem, leaf, rhs):
        return pltpu.make_async_remote_copy(
            src_ref=src, dst_ref=dst, send_sem=ssem, recv_sem=rsem,
            device_id=(leaf, rhs), device_id_type=MESH,
        )

    leaves, rank, leaf_pts = bases.shape
    features = pts.shape[0]
    cols = vt.shape[0]
    scale = math.log2(math.e) / features

    barrier = pltpu.get_barrier_semaphore()
    rhs_at = [lax.rem(r + j, ydim) for j in range(ydim)]
    rhs_from = [lax.rem(r + ydim - j, ydim) for j in range(ydim)]
    partners = [(nxt, r), (prv, r)]
    partners += [(d, to) for to in rhs_at[1:]]
    up, down = lax.rem(z + 1, zdim), lax.rem(z + zdim - 1, zdim)
    partners += [(leaf_at(up, x, core), r), (leaf_at(down, x, core), r)]
    right, left = lax.rem(x + 1, xdim), lax.rem(x + xdim - 1, xdim)
    across = lax.rem(x + 2, xdim)
    partners += [(leaf_at(z, right, core), r), (leaf_at(z, left, core), r)]
    partners += [(leaf_at(z, x, 1 - core), r)]
    for who in partners:
        pl.semaphore_signal(barrier, inc=1, device_id=who, device_id_type=MESH)

    loads = [
        pltpu.make_async_copy(vt, vall.at[r], lsem.at[0]),
        pltpu.make_async_copy(bases, bv, lsem.at[1]),
        pltpu.make_async_copy(tr, tv, lsem.at[2]),
        pltpu.make_async_copy(pts, pt, lsem.at[3]),
        pltpu.make_async_copy(uc, uv, lsem.at[4]),
        pltpu.make_async_copy(lc, lv, lsem.at[5]),
    ]
    for copy in loads:
        copy.start()

    def block_of(i):
        return pl.ds(pl.multiple_of(i * leaf_pts, leaf_pts), leaf_pts)

    pl.semaphore_wait(barrier, len(partners))

    half_leaves = leaves // 2
    points_out = [
        rc(pts.at[:, block_of(r)], hp.at[0], hp_s.at[0], hp_r.at[0], prv, r),
        rc(pts.at[:, block_of(half_leaves + r)], hp.at[1], hp_s.at[1], hp_r.at[1], nxt, r),
    ]
    lists_out = [
        rc(nl, nlr.at[0], nl_s.at[0], nl_r.at[0], prv, r),
        rc(nl, nlr.at[1], nl_s.at[1], nl_r.at[1], nxt, r),
    ]
    vectors_out = [
        rc(vt, vall.at[r], v_s.at[j - 1], v_r.at[j - 1], d, rhs_at[j]) for j in range(1, ydim)
    ]
    for copy in vectors_out + points_out + lists_out:
        copy.start()

    loads[0].wait()
    loads[1].wait()
    loads[2].wait()
    coeffs = []
    for i in range(leaves):
        bh, bl = split(bv[i])
        v = vall[r, :, block_of(i)]
        coeffs.append(mm(v, bh, NT) + mm(v, bl, NT))
    parents = []
    for i in range(leaves):
        th, tl = split(tv[i])
        ch, cl = split(coeffs[i])
        lifted = mm(ch, th) + (mm(cl, th) + mm(ch, tl))
        if i % 2 == 0:
            parents.append(lifted)
        else:
            parents[-1] = parents[-1] + lifted
    parts = coeffs + parents
    for m in range(len(parts) // 2):
        gat[z, x, core, m] = jnp.concatenate(parts[2 * m : 2 * m + 2], axis=1).astype(BF16)

    nl_own = nl[...]
    lane = lax.broadcasted_iota(jnp.int32, (leaves, 128), 1) + (d - 1) * leaves

    def mask_of(lists):
        total = jnp.zeros((leaves, 128), F32)
        for k in range(lists.shape[1]):
            entry = lists[:, k : k + 1]
            total = total + jnp.where((entry == lane) & (entry >= 0), 1.0, 0.0).astype(F32)
        return total

    masks[2] = mask_of(nl_own)
    lane_half = lax.broadcasted_iota(jnp.int32, (cols, 128), 1)
    halves[0] = jnp.where(lane_half < rank, 1.0, 0.0).astype(BF16)
    halves[1] = jnp.where(lane_half < rank, 0.0, 1.0).astype(BF16)

    top = zdim // 2
    z_out = []

    def z_send(s, to):
        block = gat.at[lax.rem(z + zdim - s, zdim), x, core]
        target = up if to <= top else down
        copy = rc(block, block, z_s.at[to], z_r.at[to], leaf_at(target, x, core), r)
        copy.start()
        z_out.append(copy)

    z_send(0, 1)
    z_send(0, zdim - 1)

    x_out = []
    steps = sorted(range(zdim), key=lambda s: (min(s, zdim - s), s))

    def x_send(s, column, kind, target):
        block = gat.at[lax.rem(z + zdim - s, zdim), column, core]
        copy = rc(block, block, x_s.at[s, kind], x_r.at[s, kind], leaf_at(z, target, core), r)
        copy.start()
        x_out.append(copy)

    def x_wait(s, column, kind):
        block = gat.at[lax.rem(z + zdim - s, zdim), column, core]
        rc(block, block, x_s.at[s, kind], x_r.at[s, kind], d, r).wait_recv()

    def z_forward(s):
        block = gat.at[lax.rem(z + zdim - s, zdim), x, core]
        rc(block, block, z_s.at[s], z_r.at[s], d, r).wait_recv()
        if s < top:
            z_send(s, s + 1)
        elif s > top + 1:
            z_send(s, s - 1)

    def x_forward(s):
        x_send(s, x, 0, right)
        x_send(s, x, 1, left)
        to_sibling(s, x, 3)

    c_out = []

    def to_sibling(s, column, kind):
        block = gat.at[lax.rem(z + zdim - s, zdim), column, core]
        copy = rc(block, block, c_s.at[s, kind], c_r.at[s, kind], leaf_at(z, x, 1 - core), r)
        copy.start()
        c_out.append(copy)

    def relay(m):
        s = steps[m]
        if m % 2 == 0:
            x_wait(s, left, 0)
            x_send(s, left, 2, right)
            to_sibling(s, left, 0)
        else:
            x_wait(s, right, 1)
            x_send(s, right, 2, left)
            to_sibling(s, right, 1)

    loads[3].wait()

    def norms(index, block):
        wide = block.astype(F32)
        row = jnp.sum(wide * wide, axis=0, keepdims=True) * (-scale)
        nrow[index] = row
        if index < leaves:
            ncol[index] = jnp.transpose(jnp.broadcast_to(row, (128, leaf_pts)))

    for i in range(leaves):
        norms(i, pt[:, block_of(i)])

    for i in range(leaves):
        acc[i] = jnp.zeros((ydim, cols, leaf_pts), F32)
    hacc[...] = jnp.zeros((2, ydim * cols, leaf_pts), F32)

    lane1 = lax.broadcasted_iota(jnp.int32, (1, 128), 1)

    def mask_at(which, row, w):
        values = masks[which, pl.ds(row, 1), :]
        return jnp.sum(jnp.where(lane1 == w, values, 0.0), axis=1, keepdims=True).astype(BF16)

    def tile_of(xa, xb, ia, ib):
        cross = mm(xa, xb)
        col = ncol[ia]
        return jnp.exp2(cross * (2.0 * scale) + (jnp.concatenate([col, col], axis=1) + nrow[ib])).astype(BF16)

    wide = (ydim * cols, leaf_pts)

    def add(i, value):
        acc[i] = acc[i] + value.reshape(ydim, cols, leaf_pts)

    def pair(t):
        a = 2 * r + t % 2 if t < leaves else r
        return a, lax.rem(a + t // 2, leaves)

    def own_tile(t):
        a, b = pair(t)
        tiles[t] = tile_of(pv[a], pt[:, block_of(b)], a, b)

    def own_products(t):
        a, b = pair(t)
        vb = vall[:, :, block_of(b)].reshape(wide)
        add(a, mm(vb * mask_at(2, a, leaves + b), tiles[t], NT))
        if t // 2:
            va = vall[:, :, block_of(a)].reshape(wide)
            add(b, mm(va * mask_at(2, b, leaves + a), tiles[t], NN))

    for i in range(leaves):
        pv[i] = jnp.transpose(pt[:, block_of(i)])
    for t in range(leaves + 1):
        own_tile(t)
        if t == 5:
            z_forward(steps[1])
            z_forward(steps[2])
    for m in range(3):
        x_forward(steps[m])

    def widen(dst, src, i):
        for k in range(8):
            w = src[i * 8 + k]
            dst[i, :, 2 * rank * k : 2 * rank * (k + 1)] = jnp.concatenate([w, w], axis=1).astype(BF16)

    loads[4].wait()
    for q in range(leaves // 2):
        widen(wu, uv, q)
    z_forward(steps[3])
    z_forward(steps[4])

    for h in range(2):
        points_out[h].wait_recv()
        norms(leaves + h, hp[h])

    def halo_of(p):
        side = lax.div(p + r, leaves)
        return side, p + r - half_leaves * side

    for p in range(leaves + 1):
        side, o = halo_of(p)
        tiles[leaves + 1 + p] = tile_of(pv[o], hp[side], o, leaves + side)
        if p == 3:
            x_forward(steps[3])
            x_forward(steps[4])
        if p == 5:
            relay(0)

    for h in range(2):
        lists_out[h].wait_recv()
        masks[h] = mask_of(nlr[h])
    z_forward(steps[5])
    z_forward(steps[6])
    x_forward(steps[5])
    x_forward(steps[6])
    for j in range(1, ydim):
        rc(vt, vall.at[rhs_from[j]], v_s.at[j - 1], v_r.at[j - 1], d, r).wait_recv()
    hv_out = [
        rc(vall.at[:, :, block_of(r)], hv.at[0], hv_s.at[0], hv_r.at[0], prv, r),
        rc(vall.at[:, :, block_of(half_leaves + r)], hv.at[1], hv_s.at[1], hv_r.at[1], nxt, r),
    ]
    for copy in hv_out:
        copy.start()

    def halo_in(p):
        side, o = halo_of(p)
        vh = hv[side].reshape(wide)
        add(o, mm(vh * mask_at(2, o, 2 * leaves + r - (leaves + half_leaves) * side), tiles[leaves + 1 + p], NT))

    def halo_back(p):
        side, o = halo_of(p)
        vo = vall[:, :, block_of(o)].reshape(wide)
        hacc[side] = hacc[side] + mm(vo * mask_at(side, r + half_leaves * side, leaves + o), tiles[leaves + 1 + p])

    for p in range(leaves + 1):
        halo_back(p)
    hsend[...] = hacc[...].reshape(2, ydim, cols, leaf_pts).astype(BF16)
    own_products(0)
    own_products(1)
    hs_out = [
        rc(hsend.at[0], hres.at[0], hs_s.at[0], hs_r.at[0], nxt, r),
        rc(hsend.at[1], hres.at[1], hs_s.at[1], hs_r.at[1], prv, r),
    ]
    for copy in hs_out:
        copy.start()
    relay(1)
    relay(2)
    for t in range(2, leaves + 1):
        own_products(t)
    z_forward(steps[7])
    x_forward(steps[7])
    for h in range(2):
        hv_out[h].wait_recv()

    a_out = []

    def wave(w):
        hs_out[w].wait_recv()
        acc[r + half_leaves * w] = acc[r + half_leaves * w] + hres[w].astype(F32)
        for j in (2, 1, 3):
            for i in range(half_leaves):
                asend[j - 1, w, i] = acc[half_leaves * w + i, rhs_at[j]].astype(BF16)

    def wave_start(w):
        for j in (2, 1, 3):
            copy = rc(
                asend.at[j - 1, w], arecv.at[j - 1, w], a_s.at[j - 1, w], a_r.at[j - 1, w], d, rhs_at[j]
            )
            copy.start()
            a_out.append(copy)

    for p in range(half_leaves):
        halo_in(p)
    wave(0)
    halo_in(half_leaves)
    wave_start(0)
    for p in range(half_leaves + 1, leaves + 1):
        halo_in(p)
    wave(1)
    loads[5].wait()
    widen(wl, lv, 0)
    wave_start(1)
    relay(3)
    relay(4)
    for i in range(1, leaves):
        widen(wl, lv, i)
    relay(5)
    relay(6)
    relay(7)

    for m in range(zdim):
        if m % 2:
            x_wait(steps[m], left, 0)
            to_sibling(steps[m], left, 0)
        else:
            x_wait(steps[m], right, 1)
            to_sibling(steps[m], right, 1)
        x_wait(steps[m], across, 2)
        to_sibling(steps[m], across, 2)
    for copy in a_out:
        copy.wait_recv()
    for i in range(leaves):
        w, e = i // half_leaves, i % half_leaves
        near = acc[i, r]
        for j in range(ydim - 1):
            near = near + arecv[j, w, e].astype(F32)
        out[:, block_of(i)] = near + RIDGE * vall[r, :, block_of(i)].astype(F32)
    for s in steps:
        for kind, column in enumerate((left, right, across, x)):
            block = gat.at[lax.rem(z + zdim - s, zdim), column, 1 - core]
            rc(block, block, c_s.at[s, kind], c_r.at[s, kind], d, r).wait_recv()

    def gathered(index, per_device, first):
        device = lax.div(index, per_device)
        inner = lax.rem(index, per_device)
        block = gat[
            lax.div(device, 2 * xdim), lax.rem(lax.div(device, 2), xdim), lax.rem(device, 2), first + lax.div(inner, 2)
        ]
        return block * halves[lax.rem(inner, 2)]

    for q in range(leaves // 2):
        left = jnp.concatenate([gathered(fu[q, k], leaves // 2, leaves // 2) for k in range(8)], axis=1)
        upper = mm(left, wu[q], NT)
        uh, ul = split(upper)
        for i in (2 * q, 2 * q + 1):
            left = jnp.concatenate([gathered(fl[i, k], leaves, 0) for k in range(8)], axis=1)
            th, tl = split(tv[i])
            field = mm(left, wl[i], NT) + (mm(uh, th, NT) + mm(ul, th, NT) + mm(uh, tl, NT))
            fh, fo = split(field)
            bh, bl = split(bv[i])
            far = mm(fh, bh) + (mm(fo, bh) + mm(fh, bl))
            out[:, block_of(i)] = out[:, block_of(i)] + far

    for copy in vectors_out + points_out + lists_out + hv_out + hs_out + a_out + x_out + c_out + z_out:
        copy.wait_send()


def solution(mesh):
    n = mesh.shape["leaf"]
    ydim = mesh.shape["rhs"]
    xdim = 4 if n >= 32 else 2
    zdim = n // (2 * xdim)

    def local(points, vectors, bases, leaf_coupling, transfer, up_coupling, far_leaf, far_up, near_lists):
        leaves, leaf_pts, rank = bases.shape
        cols = vectors.shape[1]
        features = points.shape[1]
        anywhere = pl.BlockSpec(memory_space=pl.ANY)
        vmem = pl.BlockSpec(memory_space=pltpu.VMEM)
        smem = pl.BlockSpec(memory_space=pltpu.SMEM)
        dma = pltpu.SemaphoreType.DMA
        wide = ydim * cols
        outT = pl.pallas_call(
            functools.partial(kernel, (zdim, xdim, ydim)),
            out_shape=jax.ShapeDtypeStruct((cols, leaves * leaf_pts), F32),
            in_specs=[anywhere] * 6 + [smem, smem, vmem],
            out_specs=vmem,
            scratch_shapes=[
                pltpu.VMEM((features, leaves * leaf_pts), BF16),
                pltpu.VMEM((leaves, leaf_pts, features), BF16),
                pltpu.VMEM((2, features, leaf_pts), BF16),
                pltpu.VMEM((ydim, cols, leaves * leaf_pts), BF16),
                pltpu.VMEM((2, ydim, cols, leaf_pts), BF16),
                pltpu.VMEM((2,) + near_lists.shape, jnp.int32),
                pltpu.VMEM((3, leaves, 128), F32),
                pltpu.VMEM((leaves, rank, leaf_pts), F32),
                pltpu.VMEM((leaves * 8, rank, rank), F32),
                pltpu.VMEM(transfer.shape, F32),
                pltpu.VMEM((leaves * 4, rank, rank), F32),
                pltpu.VMEM((zdim, xdim, 2, leaves * 3 // 4, cols, 2 * rank), BF16),
                pltpu.VMEM((leaves, rank, 16 * rank), BF16),
                pltpu.VMEM((leaves // 2, rank, 16 * rank), BF16),
                pltpu.VMEM((2, cols, 2 * rank), BF16),
                pltpu.VMEM((leaves + 2, leaf_pts, 128), F32),
                pltpu.VMEM((leaves + 2, 1, leaf_pts), F32),
                pltpu.VMEM((2 * leaves + 2, leaf_pts, leaf_pts), BF16),
                pltpu.VMEM((leaves, ydim, cols, leaf_pts), F32),
                pltpu.VMEM((2, wide, leaf_pts), F32),
                pltpu.VMEM((2, ydim, cols, leaf_pts), BF16),
                pltpu.VMEM((2, ydim, cols, leaf_pts), BF16),
                pltpu.VMEM((ydim - 1, 2, leaves // 2, cols, leaf_pts), BF16),
                pltpu.VMEM((ydim - 1, 2, leaves // 2, cols, leaf_pts), BF16),
                dma((6,)),
                dma((2,)), dma((2,)),
                dma((ydim - 1,)), dma((ydim - 1,)),
                dma((2,)), dma((2,)),
                dma((2,)), dma((2,)),
                dma((zdim,)), dma((zdim,)),
                dma((zdim, 3)), dma((zdim, 3)),
                dma((zdim, 4)), dma((zdim, 4)),
                dma((2,)), dma((2,)),
                dma((ydim - 1, 2)), dma((ydim - 1, 2)),
            ],
            compiler_params=pltpu.CompilerParams(
                collective_id=0, has_side_effects=True, vmem_limit_bytes=56 * 1024 * 1024
            ),
        )(
            points.T,
            vectors.T,
            jnp.transpose(bases, (0, 2, 1)),
            leaf_coupling.reshape(-1, rank, rank),
            transfer,
            up_coupling.reshape(-1, rank, rank),
            far_leaf,
            far_up,
            near_lists,
        )
        return outT.T

    return jax.shard_map(
        local,
        mesh=mesh,
        in_specs=(
            P("leaf", None),
            P("leaf", "rhs"),
            P("leaf", None, None),
            P("leaf", None, None, None),
            P("leaf", None, None),
            P("leaf", None, None, None),
            P("leaf", None),
            P("leaf", None),
            P("leaf", None),
        ),
        out_specs=P("leaf", "rhs"),
        check_vma=False,
    )
```

```python
import functools
import math

import jax
import jax.numpy as jnp
from jax import lax
from jax.experimental import pallas as pl
from jax.experimental.pallas import tpu as pltpu
from jax.sharding import PartitionSpec as P

MESH = pl.DeviceIdType.MESH
F32 = jnp.float32
BF16 = jnp.bfloat16
RIDGE = 0.5
NN = (((1,), (0,)), ((), ()))
NT = (((1,), (1,)), ((), ()))


def mm(a, b, dims=NN):
    return lax.dot_general(a, b, dims, preferred_element_type=F32)


def split(w):
    high = w.astype(BF16)
    return high, (w - high.astype(F32)).astype(BF16)


def kernel(
    dims,
    pts, vt, bases, lc, tr, uc, fl_in, fu_in, nl,
    out,
    pt, pv, hp, vall, hv, nlr, masks, bv, lv, tv, uv, gat, wl, wu, halves,
    ncol, nrow, tiles, acc, hacc, hsend, hres, asend, arecv,
    fl, fu, nlo, lsem, hp_s, hp_r, v_s, v_r, nl_s, nl_r, hv_s, hv_r, z_s, z_r, x_s, x_r, c_s, c_r, hs_s, hs_r, a_s, a_r,
):
    zdim, xdim, ydim = dims
    n = zdim * xdim * 2
    d = lax.axis_index("leaf")
    r = lax.axis_index("rhs")
    core = lax.rem(d, 2)
    x = lax.rem(lax.div(d, 2), xdim)
    z = lax.div(d, 2 * xdim)
    nxt = lax.rem(d + 1, n)
    prv = lax.rem(d + n - 1, n)

    def leaf_at(zz, xx, cc):
        return (zz * xdim + xx) * 2 + cc

    def rc(src, dst, ssem, rsem, leaf, rhs):
        return pltpu.make_async_remote_copy(
            src_ref=src, dst_ref=dst, send_sem=ssem, recv_sem=rsem,
            device_id=(leaf, rhs), device_id_type=MESH,
        )

    leaves, rank, leaf_pts = bases.shape
    features = pts.shape[0]
    cols = vt.shape[0]
    scale = math.log2(math.e) / features

    barrier = pltpu.get_barrier_semaphore()
    rhs_at = [lax.rem(r + j, ydim) for j in range(ydim)]
    rhs_from = [lax.rem(r + ydim - j, ydim) for j in range(ydim)]
    partners = [(nxt, r), (prv, r)]
    partners += [(d, to) for to in rhs_at[1:]]
    up, down = lax.rem(z + 1, zdim), lax.rem(z + zdim - 1, zdim)
    partners += [(leaf_at(up, x, core), r), (leaf_at(down, x, core), r)]
    right, left = lax.rem(x + 1, xdim), lax.rem(x + xdim - 1, xdim)
    across = lax.rem(x + 2, xdim)
    partners += [(leaf_at(z, right, core), r), (leaf_at(z, left, core), r)]
    partners += [(leaf_at(z, x, 1 - core), r)]
    for who in partners:
        pl.semaphore_signal(barrier, inc=1, device_id=who, device_id_type=MESH)

    loads = [
        pltpu.make_async_copy(vt, vall.at[r], lsem.at[0]),
        pltpu.make_async_copy(bases, bv, lsem.at[1]),
        pltpu.make_async_copy(tr, tv, lsem.at[2]),
        pltpu.make_async_copy(pts, pt, lsem.at[3]),
        pltpu.make_async_copy(uc, uv, lsem.at[4]),
        pltpu.make_async_copy(lc, lv, lsem.at[5]),
        pltpu.make_async_copy(nl, nlo, lsem.at[6]),
        pltpu.make_async_copy(fl_in, fl, lsem.at[7]),
        pltpu.make_async_copy(fu_in, fu, lsem.at[8]),
    ]
    for copy in loads:
        copy.start()

    def block_of(i):
        return pl.ds(pl.multiple_of(i * leaf_pts, leaf_pts), leaf_pts)

    pl.semaphore_wait(barrier, len(partners))

    half_leaves = leaves // 2
    points_out = [
        rc(pts.at[:, block_of(r)], hp.at[0], hp_s.at[0], hp_r.at[0], prv, r),
        rc(pts.at[:, block_of(half_leaves + r)], hp.at[1], hp_s.at[1], hp_r.at[1], nxt, r),
    ]
    lists_out = [
        rc(nl, nlr.at[0], nl_s.at[0], nl_r.at[0], prv, r),
        rc(nl, nlr.at[1], nl_s.at[1], nl_r.at[1], nxt, r),
    ]
    vectors_out = [
        rc(vt, vall.at[r], v_s.at[j - 1], v_r.at[j - 1], d, rhs_at[j]) for j in range(1, ydim)
    ]
    for copy in vectors_out + points_out + lists_out:
        copy.start()

    loads[0].wait()
    loads[1].wait()
    loads[2].wait()
    coeffs = []
    for i in range(leaves):
        bh, bl = split(bv[i])
        v = vall[r, :, block_of(i)]
        coeffs.append(mm(v, bh, NT) + mm(v, bl, NT))
    parents = []
    for i in range(leaves):
        th, tl = split(tv[i])
        ch, cl = split(coeffs[i])
        lifted = mm(ch, th) + (mm(cl, th) + mm(ch, tl))
        if i % 2 == 0:
            parents.append(lifted)
        else:
            parents[-1] = parents[-1] + lifted
    parts = coeffs + parents
    for m in range(len(parts) // 2):
        gat[z, x, core, m] = jnp.concatenate(parts[2 * m : 2 * m + 2], axis=1).astype(BF16)

    loads[6].wait()
    nl_own = nlo[...]
    lane = lax.broadcasted_iota(jnp.int32, (leaves, 128), 1) + (d - 1) * leaves

    def mask_of(lists):
        total = jnp.zeros((leaves, 128), F32)
        for k in range(lists.shape[1]):
            entry = lists[:, k : k + 1]
            total = total + jnp.where((entry == lane) & (entry >= 0), 1.0, 0.0).astype(F32)
        return total

    masks[2] = mask_of(nl_own)
    lane_half = lax.broadcasted_iota(jnp.int32, (cols, 128), 1)
    halves[0] = jnp.where(lane_half < rank, 1.0, 0.0).astype(BF16)
    halves[1] = jnp.where(lane_half < rank, 0.0, 1.0).astype(BF16)

    top = zdim // 2
    z_out = []

    def z_send(s, to):
        block = gat.at[lax.rem(z + zdim - s, zdim), x, core]
        target = up if to <= top else down
        copy = rc(block, block, z_s.at[to], z_r.at[to], leaf_at(target, x, core), r)
        copy.start()
        z_out.append(copy)

    z_send(0, 1)
    z_send(0, zdim - 1)

    x_out = []
    steps = sorted(range(zdim), key=lambda s: (min(s, zdim - s), s))

    def x_send(s, column, kind, target):
        block = gat.at[lax.rem(z + zdim - s, zdim), column, core]
        copy = rc(block, block, x_s.at[s, kind], x_r.at[s, kind], leaf_at(z, target, core), r)
        copy.start()
        x_out.append(copy)

    def x_wait(s, column, kind):
        block = gat.at[lax.rem(z + zdim - s, zdim), column, core]
        rc(block, block, x_s.at[s, kind], x_r.at[s, kind], d, r).wait_recv()

    def z_forward(s):
        block = gat.at[lax.rem(z + zdim - s, zdim), x, core]
        rc(block, block, z_s.at[s], z_r.at[s], d, r).wait_recv()
        if s < top:
            z_send(s, s + 1)
        elif s > top + 1:
            z_send(s, s - 1)

    def x_forward(s):
        x_send(s, x, 0, right)
        x_send(s, x, 1, left)
        to_sibling(s, x, 3)

    c_out = []

    def to_sibling(s, column, kind):
        block = gat.at[lax.rem(z + zdim - s, zdim), column, core]
        copy = rc(block, block, c_s.at[s, kind], c_r.at[s, kind], leaf_at(z, x, 1 - core), r)
        copy.start()
        c_out.append(copy)

    def relay(m):
        s = steps[m]
        if m % 2 == 0:
            x_wait(s, left, 0)
            x_send(s, left, 2, right)
            to_sibling(s, left, 0)
        else:
            x_wait(s, right, 1)
            x_send(s, right, 2, left)
            to_sibling(s, right, 1)

    loads[3].wait()

    def norms(index, block):
        wide = block.astype(F32)
        row = jnp.sum(wide * wide, axis=0, keepdims=True) * (-scale)
        nrow[index] = row
        if index < leaves:
            ncol[index] = jnp.transpose(jnp.broadcast_to(row, (128, leaf_pts)))

    for i in range(leaves):
        norms(i, pt[:, block_of(i)])

    for i in range(leaves):
        acc[i] = jnp.zeros((ydim, cols, leaf_pts), F32)
    hacc[...] = jnp.zeros((2, ydim * cols, leaf_pts), F32)

    lane1 = lax.broadcasted_iota(jnp.int32, (1, 128), 1)

    def mask_at(which, row, w):
        values = masks[which, pl.ds(row, 1), :]
        return jnp.sum(jnp.where(lane1 == w, values, 0.0), axis=1, keepdims=True).astype(BF16)

    def tile_of(xa, xb, ia, ib):
        cross = mm(xa, xb)
        col = ncol[ia]
        return jnp.exp2(cross * (2.0 * scale) + (jnp.concatenate([col, col], axis=1) + nrow[ib])).astype(BF16)

    wide = (ydim * cols, leaf_pts)

    def add(i, value):
        acc[i] = acc[i] + value.reshape(ydim, cols, leaf_pts)

    def pair(t):
        a = 2 * r + t % 2 if t < leaves else r
        return a, lax.rem(a + t // 2, leaves)

    def own_tile(t):
        a, b = pair(t)
        tiles[t] = tile_of(pv[a], pt[:, block_of(b)], a, b)

    def own_products(t):
        a, b = pair(t)
        vb = vall[:, :, block_of(b)].reshape(wide)
        add(a, mm(vb * mask_at(2, a, leaves + b), tiles[t], NT))
        if t // 2:
            va = vall[:, :, block_of(a)].reshape(wide)
            add(b, mm(va * mask_at(2, b, leaves + a), tiles[t], NN))

    for i in range(leaves):
        pv[i] = jnp.transpose(pt[:, block_of(i)])
    for t in range(leaves + 1):
        own_tile(t)
        if t == 5:
            z_forward(steps[1])
            z_forward(steps[2])
    for m in range(3):
        x_forward(steps[m])

    def widen(dst, src, i):
        for k in range(8):
            w = src[i * 8 + k]
            dst[i, :, 2 * rank * k : 2 * rank * (k + 1)] = jnp.concatenate([w, w], axis=1).astype(BF16)

    loads[4].wait()
    for q in range(leaves // 2):
        widen(wu, uv, q)
    for h in range(2):
        points_out[h].wait_recv()
        norms(leaves + h, hp[h])

    def halo_of(p):
        side = lax.div(p + r, leaves)
        return side, p + r - half_leaves * side

    for p in range(leaves + 1):
        side, o = halo_of(p)
        tiles[leaves + 1 + p] = tile_of(pv[o], hp[side], o, leaves + side)
        if p == 2:
            z_forward(steps[3])
            z_forward(steps[4])
            x_forward(steps[3])
            x_forward(steps[4])
        if p == 5:
            relay(0)

    for h in range(2):
        lists_out[h].wait_recv()
        masks[h] = mask_of(nlr[h])
    for j in range(1, ydim):
        rc(vt, vall.at[rhs_from[j]], v_s.at[j - 1], v_r.at[j - 1], d, r).wait_recv()
    hv_out = [
        rc(vall.at[:, :, block_of(r)], hv.at[0], hv_s.at[0], hv_r.at[0], prv, r),
        rc(vall.at[:, :, block_of(half_leaves + r)], hv.at[1], hv_s.at[1], hv_r.at[1], nxt, r),
    ]
    for copy in hv_out:
        copy.start()

    def halo_in(p):
        side, o = halo_of(p)
        vh = hv[side].reshape(wide)
        add(o, mm(vh * mask_at(2, o, 2 * leaves + r - (leaves + half_leaves) * side), tiles[leaves + 1 + p], NT))

    def halo_back(p):
        side, o = halo_of(p)
        vo = vall[:, :, block_of(o)].reshape(wide)
        hacc[side] = hacc[side] + mm(vo * mask_at(side, r + half_leaves * side, leaves + o), tiles[leaves + 1 + p])

    for p in range(leaves + 1):
        halo_back(p)
    hsend[...] = hacc[...].reshape(2, ydim, cols, leaf_pts).astype(BF16)
    own_products(0)
    own_products(1)
    hs_out = [
        rc(hsend.at[0], hres.at[0], hs_s.at[0], hs_r.at[0], nxt, r),
        rc(hsend.at[1], hres.at[1], hs_s.at[1], hs_r.at[1], prv, r),
    ]
    for copy in hs_out:
        copy.start()
    z_forward(steps[5])
    z_forward(steps[6])
    x_forward(steps[5])
    x_forward(steps[6])
    for t in range(2, leaves + 1):
        own_products(t)
    relay(1)
    relay(2)
    for h in range(2):
        hv_out[h].wait_recv()

    a_out = []

    def wave(w):
        hs_out[w].wait_recv()
        acc[r + half_leaves * w] = acc[r + half_leaves * w] + hres[w].astype(F32)
        for j in (2, 1, 3):
            for i in range(half_leaves):
                asend[j - 1, w, i] = acc[half_leaves * w + i, rhs_at[j]].astype(BF16)

    def wave_start(w):
        for j in (2, 1, 3):
            copy = rc(
                asend.at[j - 1, w], arecv.at[j - 1, w], a_s.at[j - 1, w], a_r.at[j - 1, w], d, rhs_at[j]
            )
            copy.start()
            a_out.append(copy)

    for p in range(half_leaves):
        halo_in(p)
    wave(0)
    halo_in(half_leaves)
    wave_start(0)
    z_forward(steps[7])
    x_forward(steps[7])
    for p in range(half_leaves + 1, leaves + 1):
        halo_in(p)
    wave(1)
    loads[5].wait()
    widen(wl, lv, 0)
    wave_start(1)
    relay(3)
    relay(4)
    for i in range(1, leaves):
        widen(wl, lv, i)
    relay(5)
    relay(6)
    relay(7)

    for m in range(zdim):
        if m % 2:
            x_wait(steps[m], left, 0)
            to_sibling(steps[m], left, 0)
        else:
            x_wait(steps[m], right, 1)
            to_sibling(steps[m], right, 1)
        x_wait(steps[m], across, 2)
        to_sibling(steps[m], across, 2)
    for copy in a_out:
        copy.wait_recv()
    for i in range(leaves):
        w, e = i // half_leaves, i % half_leaves
        near = acc[i, r]
        for j in range(ydim - 1):
            near = near + arecv[j, w, e].astype(F32)
        out[:, block_of(i)] = near + RIDGE * vall[r, :, block_of(i)].astype(F32)
    for s in steps:
        for kind, column in enumerate((left, right, across, x)):
            block = gat.at[lax.rem(z + zdim - s, zdim), column, 1 - core]
            rc(block, block, c_s.at[s, kind], c_r.at[s, kind], d, r).wait_recv()

    def gathered(index, per_device, first):
        device = lax.div(index, per_device)
        inner = lax.rem(index, per_device)
        block = gat[
            lax.div(device, 2 * xdim), lax.rem(lax.div(device, 2), xdim), lax.rem(device, 2), first + lax.div(inner, 2)
        ]
        return block * halves[lax.rem(inner, 2)]

    loads[7].wait()
    loads[8].wait()
    uppers = []
    for q in range(leaves // 2):
        left_in = jnp.concatenate([gathered(fu[q, k], leaves // 2, leaves // 2) for k in range(8)], axis=1)
        uppers.append(split(mm(left_in, wu[q], NT)))
    fields = []
    for i in range(leaves):
        left_in = jnp.concatenate([gathered(fl[i, k], leaves, 0) for k in range(8)], axis=1)
        fields.append(mm(left_in, wl[i], NT))
    for i in range(leaves):
        th, tl = split(tv[i])
        uh, ul = uppers[i // 2]
        fields[i] = split(fields[i] + (mm(uh, th, NT) + mm(ul, th, NT) + mm(uh, tl, NT)))
    fars = []
    for i in range(leaves):
        fh, fo = fields[i]
        bh, bl = split(bv[i])
        fars.append(mm(fh, bh) + (mm(fo, bh) + mm(fh, bl)))
    for i in range(leaves):
        out[:, block_of(i)] = out[:, block_of(i)] + fars[i]

    for copy in vectors_out + points_out + lists_out + hv_out + hs_out + a_out + x_out + c_out + z_out:
        copy.wait_send()


def solution(mesh):
    n = mesh.shape["leaf"]
    ydim = mesh.shape["rhs"]
    xdim = 4 if n >= 32 else 2
    zdim = n // (2 * xdim)

    def local(points, vectors, bases, leaf_coupling, transfer, up_coupling, far_leaf, far_up, near_lists):
        leaves, leaf_pts, rank = bases.shape
        cols = vectors.shape[1]
        features = points.shape[1]
        anywhere = pl.BlockSpec(memory_space=pl.ANY)
        vmem = pl.BlockSpec(memory_space=pltpu.VMEM)
        dma = pltpu.SemaphoreType.DMA
        wide = ydim * cols
        outT = pl.pallas_call(
            functools.partial(kernel, (zdim, xdim, ydim)),
            out_shape=pltpu.VMEM((cols, leaves * leaf_pts), F32),
            in_specs=[anywhere] * 9,
            out_specs=vmem,
            scratch_shapes=[
                pltpu.VMEM((features, leaves * leaf_pts), BF16),
                pltpu.VMEM((leaves, leaf_pts, features), BF16),
                pltpu.VMEM((2, features, leaf_pts), BF16),
                pltpu.VMEM((ydim, cols, leaves * leaf_pts), BF16),
                pltpu.VMEM((2, ydim, cols, leaf_pts), BF16),
                pltpu.VMEM((2,) + near_lists.shape, jnp.int32),
                pltpu.VMEM((3, leaves, 128), F32),
                pltpu.VMEM((leaves, rank, leaf_pts), F32),
                pltpu.VMEM((leaves * 8, rank, rank), F32),
                pltpu.VMEM(transfer.shape, F32),
                pltpu.VMEM((leaves * 4, rank, rank), F32),
                pltpu.VMEM((zdim, xdim, 2, leaves * 3 // 4, cols, 2 * rank), BF16),
                pltpu.VMEM((leaves, rank, 16 * rank), BF16),
                pltpu.VMEM((leaves // 2, rank, 16 * rank), BF16),
                pltpu.VMEM((2, cols, 2 * rank), BF16),
                pltpu.VMEM((leaves + 2, leaf_pts, 128), F32),
                pltpu.VMEM((leaves + 2, 1, leaf_pts), F32),
                pltpu.VMEM((2 * leaves + 2, leaf_pts, leaf_pts), BF16),
                pltpu.VMEM((leaves, ydim, cols, leaf_pts), F32),
                pltpu.VMEM((2, wide, leaf_pts), F32),
                pltpu.VMEM((2, ydim, cols, leaf_pts), BF16),
                pltpu.VMEM((2, ydim, cols, leaf_pts), BF16),
                pltpu.VMEM((ydim - 1, 2, leaves // 2, cols, leaf_pts), BF16),
                pltpu.VMEM((ydim - 1, 2, leaves // 2, cols, leaf_pts), BF16),
                pltpu.SMEM(far_leaf.shape, jnp.int32),
                pltpu.SMEM(far_up.shape, jnp.int32),
                pltpu.VMEM(near_lists.shape, jnp.int32),
                dma((9,)),
                dma((2,)), dma((2,)),
                dma((ydim - 1,)), dma((ydim - 1,)),
                dma((2,)), dma((2,)),
                dma((2,)), dma((2,)),
                dma((zdim,)), dma((zdim,)),
                dma((zdim, 3)), dma((zdim, 3)),
                dma((zdim, 4)), dma((zdim, 4)),
                dma((2,)), dma((2,)),
                dma((ydim - 1, 2)), dma((ydim - 1, 2)),
            ],
            compiler_params=pltpu.CompilerParams(
                collective_id=0, has_side_effects=True, vmem_limit_bytes=56 * 1024 * 1024
            ),
        )(
            points.T,
            vectors.T,
            jnp.transpose(bases, (0, 2, 1)),
            leaf_coupling.reshape(-1, rank, rank),
            transfer,
            up_coupling.reshape(-1, rank, rank),
            far_leaf,
            far_up,
            near_lists,
        )
        return outT.T

    return jax.shard_map(
        local,
        mesh=mesh,
        in_specs=(
            P("leaf", None),
            P("leaf", "rhs"),
            P("leaf", None, None),
            P("leaf", None, None, None),
            P("leaf", None, None),
            P("leaf", None, None, None),
            P("leaf", None),
            P("leaf", None),
            P("leaf", None),
        ),
        out_specs=P("leaf", "rhs"),
        check_vma=False,
    )
```

```python
import functools
import math

import jax
import jax.numpy as jnp
from jax import lax
from jax.experimental import pallas as pl
from jax.experimental.pallas import tpu as pltpu
from jax.sharding import PartitionSpec as P

MESH = pl.DeviceIdType.MESH
F32 = jnp.float32
BF16 = jnp.bfloat16
RIDGE = 0.5
NN = (((1,), (0,)), ((), ()))
NT = (((1,), (1,)), ((), ()))


def mm(a, b, dims=NN):
    return lax.dot_general(a, b, dims, preferred_element_type=F32)


def split(w):
    high = w.astype(BF16)
    return high, (w - high.astype(F32)).astype(BF16)


def kernel(
    dims,
    pts, vt, bases, lc, tr, uc, fl_in, fu_in, nl,
    out,
    pt, pv, hp, vall, hv, nlr, masks, bv, lv, tv, uv, gat, wl, wu, halves,
    ncol, nrow, tiles, acc, hacc, hsend, hres, asend, arecv,
    fl, fu, nlo, lsem, hp_s, hp_r, v_s, v_r, nl_s, nl_r, hv_s, hv_r, z_s, z_r, x_s, x_r, c_s, c_r, hs_s, hs_r, a_s, a_r,
):
    zdim, xdim, ydim = dims
    n = zdim * xdim * 2
    d = lax.axis_index("leaf")
    r = lax.axis_index("rhs")
    core = lax.rem(d, 2)
    x = lax.rem(lax.div(d, 2), xdim)
    z = lax.div(d, 2 * xdim)
    nxt = lax.rem(d + 1, n)
    prv = lax.rem(d + n - 1, n)

    def leaf_at(zz, xx, cc):
        return (zz * xdim + xx) * 2 + cc

    def rc(src, dst, ssem, rsem, leaf, rhs):
        return pltpu.make_async_remote_copy(
            src_ref=src, dst_ref=dst, send_sem=ssem, recv_sem=rsem,
            device_id=(leaf, rhs), device_id_type=MESH,
        )

    leaves, rank, leaf_pts = bases.shape
    features = pts.shape[0]
    cols = vt.shape[0]
    scale = math.log2(math.e) / features

    barrier = pltpu.get_barrier_semaphore()
    rhs_at = [lax.rem(r + j, ydim) for j in range(ydim)]
    rhs_from = [lax.rem(r + ydim - j, ydim) for j in range(ydim)]
    partners = [(nxt, r), (prv, r)]
    partners += [(d, to) for to in rhs_at[1:]]
    up, down = lax.rem(z + 1, zdim), lax.rem(z + zdim - 1, zdim)
    partners += [(leaf_at(up, x, core), r), (leaf_at(down, x, core), r)]
    right, left = lax.rem(x + 1, xdim), lax.rem(x + xdim - 1, xdim)
    across = lax.rem(x + 2, xdim)
    partners += [(leaf_at(z, right, core), r), (leaf_at(z, left, core), r)]
    partners += [(leaf_at(z, x, 1 - core), r)]
    for who in partners:
        pl.semaphore_signal(barrier, inc=1, device_id=who, device_id_type=MESH)

    loads = [
        pltpu.make_async_copy(vt, vall.at[r], lsem.at[0]),
        pltpu.make_async_copy(bases, bv, lsem.at[1]),
        pltpu.make_async_copy(tr, tv, lsem.at[2]),
        pltpu.make_async_copy(pts, pt, lsem.at[3]),
        pltpu.make_async_copy(uc, uv, lsem.at[4]),
        pltpu.make_async_copy(lc, lv, lsem.at[5]),
        pltpu.make_async_copy(nl, nlo, lsem.at[6]),
        pltpu.make_async_copy(fl_in, fl, lsem.at[7]),
        pltpu.make_async_copy(fu_in, fu, lsem.at[8]),
    ]
    for copy in loads:
        copy.start()

    def block_of(i):
        return pl.ds(pl.multiple_of(i * leaf_pts, leaf_pts), leaf_pts)

    pl.semaphore_wait(barrier, len(partners))

    half_leaves = leaves // 2
    points_out = [
        rc(pts.at[:, block_of(r)], hp.at[0], hp_s.at[0], hp_r.at[0], prv, r),
        rc(pts.at[:, block_of(half_leaves + r)], hp.at[1], hp_s.at[1], hp_r.at[1], nxt, r),
    ]
    lists_out = [
        rc(nl, nlr.at[0], nl_s.at[0], nl_r.at[0], prv, r),
        rc(nl, nlr.at[1], nl_s.at[1], nl_r.at[1], nxt, r),
    ]
    vectors_out = [
        rc(vt, vall.at[r], v_s.at[j - 1], v_r.at[j - 1], d, rhs_at[j]) for j in range(1, ydim)
    ]
    for copy in vectors_out + points_out + lists_out:
        copy.start()

    loads[0].wait()
    loads[1].wait()
    loads[2].wait()
    coeffs = []
    for i in range(leaves):
        bh, bl = split(bv[i])
        v = vall[r, :, block_of(i)]
        coeffs.append(mm(v, bh, NT) + mm(v, bl, NT))
    parents = []
    for i in range(leaves):
        th, tl = split(tv[i])
        ch, cl = split(coeffs[i])
        lifted = mm(ch, th) + (mm(cl, th) + mm(ch, tl))
        if i % 2 == 0:
            parents.append(lifted)
        else:
            parents[-1] = parents[-1] + lifted
    parts = coeffs + parents
    for m in range(len(parts) // 2):
        gat[z, x, core, m] = jnp.concatenate(parts[2 * m : 2 * m + 2], axis=1).astype(BF16)

    loads[6].wait()
    nl_own = nlo[...]
    lane = lax.broadcasted_iota(jnp.int32, (leaves, 128), 1) + (d - 1) * leaves

    def mask_of(lists):
        total = jnp.zeros((leaves, 128), F32)
        for k in range(lists.shape[1]):
            entry = lists[:, k : k + 1]
            total = total + jnp.where((entry == lane) & (entry >= 0), 1.0, 0.0).astype(F32)
        return total

    masks[2] = mask_of(nl_own)
    lane_half = lax.broadcasted_iota(jnp.int32, (cols, 128), 1)
    halves[0] = jnp.where(lane_half < rank, 1.0, 0.0).astype(BF16)
    halves[1] = jnp.where(lane_half < rank, 0.0, 1.0).astype(BF16)

    top = zdim // 2
    z_out = []

    def z_send(s, to):
        block = gat.at[lax.rem(z + zdim - s, zdim), x, core]
        target = up if to <= top else down
        copy = rc(block, block, z_s.at[to], z_r.at[to], leaf_at(target, x, core), r)
        copy.start()
        z_out.append(copy)

    z_send(0, 1)
    z_send(0, zdim - 1)

    x_out = []
    steps = sorted(range(zdim), key=lambda s: (min(s, zdim - s), s))

    def x_send(s, column, kind, target):
        block = gat.at[lax.rem(z + zdim - s, zdim), column, core]
        copy = rc(block, block, x_s.at[s, kind], x_r.at[s, kind], leaf_at(z, target, core), r)
        copy.start()
        x_out.append(copy)

    def x_wait(s, column, kind):
        block = gat.at[lax.rem(z + zdim - s, zdim), column, core]
        rc(block, block, x_s.at[s, kind], x_r.at[s, kind], d, r).wait_recv()

    def z_forward(s):
        block = gat.at[lax.rem(z + zdim - s, zdim), x, core]
        rc(block, block, z_s.at[s], z_r.at[s], d, r).wait_recv()
        if s < top:
            z_send(s, s + 1)
        elif s > top + 1:
            z_send(s, s - 1)

    def x_forward(s):
        x_send(s, x, 0, right)
        x_send(s, x, 1, left)
        to_sibling(s, x, 3)

    c_out = []

    def to_sibling(s, column, kind):
        block = gat.at[lax.rem(z + zdim - s, zdim), column, core]
        copy = rc(block, block, c_s.at[s, kind], c_r.at[s, kind], leaf_at(z, x, 1 - core), r)
        copy.start()
        c_out.append(copy)

    def relay(m):
        s = steps[m]
        if m % 2 == 0:
            x_wait(s, left, 0)
            x_send(s, left, 2, right)
            to_sibling(s, left, 0)
        else:
            x_wait(s, right, 1)
            x_send(s, right, 2, left)
            to_sibling(s, right, 1)

    loads[3].wait()

    def norms(index, block):
        wide = block.astype(F32)
        row = jnp.sum(wide * wide, axis=0, keepdims=True) * (-scale)
        nrow[index] = row
        if index < leaves:
            ncol[index] = jnp.transpose(jnp.broadcast_to(row, (128, leaf_pts)))

    for i in range(leaves):
        norms(i, pt[:, block_of(i)])

    for i in range(leaves):
        acc[i] = jnp.zeros((ydim, cols, leaf_pts), F32)
    hacc[...] = jnp.zeros((2, ydim * cols, leaf_pts), F32)

    lane1 = lax.broadcasted_iota(jnp.int32, (1, 128), 1)

    def mask_at(which, row, w):
        values = masks[which, pl.ds(row, 1), :]
        return jnp.sum(jnp.where(lane1 == w, values, 0.0), axis=1, keepdims=True).astype(BF16)

    def tile_of(xa, xb, ia, ib):
        cross = mm(xa, xb)
        col = ncol[ia]
        return jnp.exp2(cross * (2.0 * scale) + (jnp.concatenate([col, col], axis=1) + nrow[ib])).astype(BF16)

    wide = (ydim * cols, leaf_pts)

    def add(i, value):
        acc[i] = acc[i] + value.reshape(ydim, cols, leaf_pts)

    def pair(t):
        a = 2 * r + t % 2 if t < leaves else r
        return a, lax.rem(a + t // 2, leaves)

    def own_tile(t):
        a, b = pair(t)
        tiles[t] = tile_of(pv[a], pt[:, block_of(b)], a, b)

    def own_products(t):
        a, b = pair(t)
        vb = vall[:, :, block_of(b)].reshape(wide)
        add(a, mm(vb * mask_at(2, a, leaves + b), tiles[t], NT))
        if t // 2:
            va = vall[:, :, block_of(a)].reshape(wide)
            add(b, mm(va * mask_at(2, b, leaves + a), tiles[t], NN))

    for i in range(leaves):
        pv[i] = jnp.transpose(pt[:, block_of(i)])
    for t in range(leaves + 1):
        own_tile(t)
        if t == 5:
            z_forward(steps[1])
            z_forward(steps[2])
    for m in range(3):
        x_forward(steps[m])

    def widen(dst, src, i):
        for k in range(8):
            w = src[i * 8 + k]
            dst[i, :, 2 * rank * k : 2 * rank * (k + 1)] = jnp.concatenate([w, w], axis=1).astype(BF16)

    loads[4].wait()
    for q in range(leaves // 2):
        widen(wu, uv, q)
    for h in range(2):
        points_out[h].wait_recv()
        norms(leaves + h, hp[h])

    def halo_of(p):
        side = lax.div(p + r, leaves)
        return side, p + r - half_leaves * side

    for p in range(leaves + 1):
        side, o = halo_of(p)
        tiles[leaves + 1 + p] = tile_of(pv[o], hp[side], o, leaves + side)
        if p == 2:
            z_forward(steps[3])
            z_forward(steps[4])
            x_forward(steps[3])
            x_forward(steps[4])
        if p == 5:
            relay(0)

    for h in range(2):
        lists_out[h].wait_recv()
        masks[h] = mask_of(nlr[h])
    for j in range(1, ydim):
        rc(vt, vall.at[rhs_from[j]], v_s.at[j - 1], v_r.at[j - 1], d, r).wait_recv()
    hv_out = [
        rc(vall.at[:, :, block_of(r)], hv.at[0], hv_s.at[0], hv_r.at[0], prv, r),
        rc(vall.at[:, :, block_of(half_leaves + r)], hv.at[1], hv_s.at[1], hv_r.at[1], nxt, r),
    ]
    for copy in hv_out:
        copy.start()

    def halo_in(p):
        side, o = halo_of(p)
        vh = hv[side].reshape(wide)
        add(o, mm(vh * mask_at(2, o, 2 * leaves + r - (leaves + half_leaves) * side), tiles[leaves + 1 + p], NT))

    def halo_back(p):
        side, o = halo_of(p)
        vo = vall[:, :, block_of(o)].reshape(wide)
        hacc[side] = hacc[side] + mm(vo * mask_at(side, r + half_leaves * side, leaves + o), tiles[leaves + 1 + p])

    for p in range(leaves + 1):
        halo_back(p)
    hsend[...] = hacc[...].reshape(2, ydim, cols, leaf_pts).astype(BF16)
    own_products(0)
    own_products(1)
    hs_out = [
        rc(hsend.at[0], hres.at[0], hs_s.at[0], hs_r.at[0], nxt, r),
        rc(hsend.at[1], hres.at[1], hs_s.at[1], hs_r.at[1], prv, r),
    ]
    for copy in hs_out:
        copy.start()
    for t in range(2, leaves + 1):
        own_products(t)
    z_forward(steps[5])
    z_forward(steps[6])
    x_forward(steps[5])
    x_forward(steps[6])
    relay(1)
    relay(2)
    for h in range(2):
        hv_out[h].wait_recv()

    a_out = []

    def wave(w):
        hs_out[w].wait_recv()
        acc[r + half_leaves * w] = acc[r + half_leaves * w] + hres[w].astype(F32)
        for j in (2, 1, 3):
            for i in range(half_leaves):
                asend[j - 1, w, i] = acc[half_leaves * w + i, rhs_at[j]].astype(BF16)

    def wave_start(w):
        for j in (2, 1, 3):
            copy = rc(
                asend.at[j - 1, w], arecv.at[j - 1, w], a_s.at[j - 1, w], a_r.at[j - 1, w], d, rhs_at[j]
            )
            copy.start()
            a_out.append(copy)

    for p in range(half_leaves):
        halo_in(p)
    wave(0)
    halo_in(half_leaves)
    wave_start(0)
    z_forward(steps[7])
    x_forward(steps[7])
    for p in range(half_leaves + 1, leaves + 1):
        halo_in(p)
    wave(1)
    loads[5].wait()
    widen(wl, lv, 0)
    wave_start(1)
    relay(3)
    relay(4)
    for i in range(1, leaves):
        widen(wl, lv, i)
    relay(5)
    relay(6)
    relay(7)

    for m in range(zdim):
        if m % 2:
            x_wait(steps[m], left, 0)
            to_sibling(steps[m], left, 0)
        else:
            x_wait(steps[m], right, 1)
            to_sibling(steps[m], right, 1)
        x_wait(steps[m], across, 2)
        to_sibling(steps[m], across, 2)
    for copy in a_out:
        copy.wait_recv()
    for copy in vectors_out + points_out + lists_out + hv_out + hs_out + a_out + x_out + z_out:
        copy.wait_send()
    for i in range(leaves):
        w, e = i // half_leaves, i % half_leaves
        near = acc[i, r]
        for j in range(ydim - 1):
            near = near + arecv[j, w, e].astype(F32)
        out[:, block_of(i)] = near + RIDGE * vall[r, :, block_of(i)].astype(F32)
    for s in steps:
        for kind, column in enumerate((left, right, across, x)):
            block = gat.at[lax.rem(z + zdim - s, zdim), column, 1 - core]
            rc(block, block, c_s.at[s, kind], c_r.at[s, kind], d, r).wait_recv()

    def gathered(index, per_device, first):
        device = lax.div(index, per_device)
        inner = lax.rem(index, per_device)
        block = gat[
            lax.div(device, 2 * xdim), lax.rem(lax.div(device, 2), xdim), lax.rem(device, 2), first + lax.div(inner, 2)
        ]
        return block * halves[lax.rem(inner, 2)]

    loads[7].wait()
    loads[8].wait()
    uppers = []
    for q in range(leaves // 2):
        left_in = jnp.concatenate([gathered(fu[q, k], leaves // 2, leaves // 2) for k in range(8)], axis=1)
        uppers.append(split(mm(left_in, wu[q], NT)))
    fields = []
    for i in range(leaves):
        left_in = jnp.concatenate([gathered(fl[i, k], leaves, 0) for k in range(8)], axis=1)
        fields.append(mm(left_in, wl[i], NT))
    for i in range(leaves):
        th, tl = split(tv[i])
        uh, ul = uppers[i // 2]
        fields[i] = split(fields[i] + (mm(uh, th, NT) + mm(ul, th, NT) + mm(uh, tl, NT)))
    fars = []
    for i in range(leaves):
        fh, fo = fields[i]
        bh, bl = split(bv[i])
        fars.append(mm(fh, bh) + (mm(fo, bh) + mm(fh, bl)))
    for i in range(leaves):
        out[:, block_of(i)] = out[:, block_of(i)] + fars[i]

    for copy in c_out:
        copy.wait_send()


def solution(mesh):
    n = mesh.shape["leaf"]
    ydim = mesh.shape["rhs"]
    xdim = 4 if n >= 32 else 2
    zdim = n // (2 * xdim)

    def local(points, vectors, bases, leaf_coupling, transfer, up_coupling, far_leaf, far_up, near_lists):
        leaves, leaf_pts, rank = bases.shape
        cols = vectors.shape[1]
        features = points.shape[1]
        anywhere = pl.BlockSpec(memory_space=pl.ANY)
        vmem = pl.BlockSpec(memory_space=pltpu.VMEM)
        dma = pltpu.SemaphoreType.DMA
        wide = ydim * cols
        outT = pl.pallas_call(
            functools.partial(kernel, (zdim, xdim, ydim)),
            out_shape=pltpu.VMEM((cols, leaves * leaf_pts), F32),
            in_specs=[anywhere] * 9,
            out_specs=vmem,
            scratch_shapes=[
                pltpu.VMEM((features, leaves * leaf_pts), BF16),
                pltpu.VMEM((leaves, leaf_pts, features), BF16),
                pltpu.VMEM((2, features, leaf_pts), BF16),
                pltpu.VMEM((ydim, cols, leaves * leaf_pts), BF16),
                pltpu.VMEM((2, ydim, cols, leaf_pts), BF16),
                pltpu.VMEM((2,) + near_lists.shape, jnp.int32),
                pltpu.VMEM((3, leaves, 128), F32),
                pltpu.VMEM((leaves, rank, leaf_pts), F32),
                pltpu.VMEM((leaves * 8, rank, rank), F32),
                pltpu.VMEM(transfer.shape, F32),
                pltpu.VMEM((leaves * 4, rank, rank), F32),
                pltpu.VMEM((zdim, xdim, 2, leaves * 3 // 4, cols, 2 * rank), BF16),
                pltpu.VMEM((leaves, rank, 16 * rank), BF16),
                pltpu.VMEM((leaves // 2, rank, 16 * rank), BF16),
                pltpu.VMEM((2, cols, 2 * rank), BF16),
                pltpu.VMEM((leaves + 2, leaf_pts, 128), F32),
                pltpu.VMEM((leaves + 2, 1, leaf_pts), F32),
                pltpu.VMEM((2 * leaves + 2, leaf_pts, leaf_pts), BF16),
                pltpu.VMEM((leaves, ydim, cols, leaf_pts), F32),
                pltpu.VMEM((2, wide, leaf_pts), F32),
                pltpu.VMEM((2, ydim, cols, leaf_pts), BF16),
                pltpu.VMEM((2, ydim, cols, leaf_pts), BF16),
                pltpu.VMEM((ydim - 1, 2, leaves // 2, cols, leaf_pts), BF16),
                pltpu.VMEM((ydim - 1, 2, leaves // 2, cols, leaf_pts), BF16),
                pltpu.SMEM(far_leaf.shape, jnp.int32),
                pltpu.SMEM(far_up.shape, jnp.int32),
                pltpu.VMEM(near_lists.shape, jnp.int32),
                dma((9,)),
                dma((2,)), dma((2,)),
                dma((ydim - 1,)), dma((ydim - 1,)),
                dma((2,)), dma((2,)),
                dma((2,)), dma((2,)),
                dma((zdim,)), dma((zdim,)),
                dma((zdim, 3)), dma((zdim, 3)),
                dma((zdim, 4)), dma((zdim, 4)),
                dma((2,)), dma((2,)),
                dma((ydim - 1, 2)), dma((ydim - 1, 2)),
            ],
            compiler_params=pltpu.CompilerParams(
                collective_id=0, has_side_effects=True, vmem_limit_bytes=56 * 1024 * 1024
            ),
        )(
            points.T,
            vectors.T,
            jnp.transpose(bases, (0, 2, 1)),
            leaf_coupling.reshape(-1, rank, rank),
            transfer,
            up_coupling.reshape(-1, rank, rank),
            far_leaf,
            far_up,
            near_lists,
        )
        return outT.T

    return jax.shard_map(
        local,
        mesh=mesh,
        in_specs=(
            P("leaf", None),
            P("leaf", "rhs"),
            P("leaf", None, None),
            P("leaf", None, None, None),
            P("leaf", None, None),
            P("leaf", None, None, None),
            P("leaf", None),
            P("leaf", None),
            P("leaf", None),
        ),
        out_specs=P("leaf", "rhs"),
        check_vma=False,
    )
```
